32 devices in a mesh: seq: 8 (over z, core), grp: 2 (over y), dp: 2 (over x).
Axes of the slice: x: 2, y: 2, z: 4, core: 2. Of those that a mesh axis runs over, the one named last changes fastest.
Arguments:
- clips: bfloat16 [2, 1024, 1408], P('dp', 'seq'), may hold values from -6 to 6
- context: int32 [2, 1024], P('dp', 'seq'), may hold values from 0 to 1, as said below
- predict_index: int32 [2, 1536], P('dp', 'seq'), may hold values from -1 to 1023, as said below
- target_qkv: bfloat16 [3, 1408, 1408], P(None, 'dp', 'grp'), may hold values from -8 to 8
- target_out: bfloat16 [1408, 1408], P('grp'), may hold values from -0.15625 to 0.15625
- student_qkv: bfloat16 [3, 1408, 1408], P(None, 'dp', 'grp'), may hold values from -8 to 8
- student_out: bfloat16 [1408, 1408], P('grp', 'dp'), may hold values from -0.15625 to 0.15625
- mask_token: float32 [1408], replicated, may hold values from -4 to 4
Outputs:
- out_grad: float32 [1408, 1408], P('grp', 'dp')
- target_blend: float32 [1408, 1408], P('grp')
The draws below stay inside these ranges and needn't reach their ends.
Inputs may be any that keep to these rules, and one draw needn't show every extreme that they name: In every aligned block of 128 tokens of a clip exactly 32 tokens have context 1 and the others 0. `predict_index`: each device's 192 slots name distinct target positions (context 0) of its clip, followed by -1 in the unused slots; different devices' lists may name the same position. In every clip one list is full.
All inputs are finite; a program needn't handle non-finite values.
Results may differ from the reference program's by a relative error of at most 0.014.
Values may be sent and summed in bfloat16 or wider, within the bound.
A program may use at most 128 MiB of HBM per device.

```python
import math
import jax
import jax.numpy as jnp
from jax import lax

D = 1408
HEAD_DIM = 88
TOK_DEV = 128
TGT_DEV = 96
SLOTS = 192
TOKENS = 1024
CLIPS = 2
N_GRP = 2


def draw_plan(base_key):
    shard_total = TOKENS // TOK_DEV
    stream = jax.random.fold_in(base_key, 11)
    clip_keys = jax.random.split(stream, CLIPS)

    def one_clip(clip_key):
        mask_key, pick_key, load_key, busy_key = jax.random.split(clip_key, 4)
        shard_keys = jax.random.split(mask_key, shard_total)
        shuffled = jax.vmap(lambda single: jax.random.permutation(single, TOK_DEV))(shard_keys)
        is_target = (shuffled < TGT_DEV).reshape(TOKENS)
        flags = jnp.where(is_target, 0, 1).astype(jnp.int32)
        busiest = jax.random.randint(busy_key, (), 0, shard_total)
        loads = jax.random.randint(load_key, (shard_total,), TGT_DEV // 2, TGT_DEV + 1)
        devices = jnp.arange(shard_total, dtype=jnp.int32)
        counts = jnp.where(devices == busiest, SLOTS, loads).astype(jnp.int32)
        pick_keys = jax.random.split(pick_key, shard_total)

        def one_list(single, count):
            ordering = jax.random.permutation(single, TOKENS).astype(jnp.int32)
            ranking = jnp.where(is_target, ordering, TOKENS + ordering)
            chosen = jnp.argsort(ranking, stable=True)[:SLOTS].astype(jnp.int32)
            slot_ids = jnp.arange(SLOTS, dtype=jnp.int32)
            return jnp.where(slot_ids < count, chosen, -1).astype(jnp.int32)
        lists = jax.vmap(one_list)(pick_keys, counts)
        return (flags, lists.reshape(shard_total * SLOTS))
    return jax.vmap(one_clip)(clip_keys)


def mask_vector(base_key):
    return jnp.clip(jax.random.normal(jax.random.fold_in(base_key, 31), (D,), jnp.float32), -4.0, 4.0)


def draw_weights(base_key, salt):
    local_key = jax.random.fold_in(base_key, salt)
    base_key_two = jax.random.fold_in(local_key, 0)
    scale = D ** (-0.5)
    base = jnp.clip(jax.random.normal(base_key_two, (3, D, D), jnp.float32), -6.0, 6.0) * scale
    return base


def draw_target_qkv(key, part):
    return draw_weights(key, 41).astype(jnp.bfloat16)


def draw_student_qkv(key, part):
    return draw_weights(key, 43).astype(jnp.bfloat16)


def draw_mask_token(key, part):
    return mask_vector(key)


def draw_clips(key, part):
    noise_key = jax.random.fold_in(key, 37)
    first_key = jax.random.fold_in(noise_key, 0)
    base = jnp.clip(jax.random.normal(first_key, (CLIPS, TOKENS, D), jnp.float32), -5.0, 5.0)
    return base.astype(jnp.bfloat16)


def draw_context(key, part):
    return draw_plan(key)[0]


def draw_predict_index(key, part):
    return draw_plan(key)[1]


def block_levels(stream_key, dims, cuts, smallest, largest):
    def one(dim, blocks):
        draws = jax.random.uniform(jax.random.fold_in(jax.random.fold_in(stream_key, 6), dim), (blocks,), jnp.float32, smallest / len(cuts), largest / len(cuts))
        return jnp.repeat(jnp.exp(draws), dims[dim] // blocks).reshape((-1,) + (1,) * (len(dims) - dim - 1))

    loudness = one(*cuts[0])
    for cut in cuts[1:]:
        loudness = loudness * one(*cut)
    return loudness


def scatter_about(stream_key, extent, scale, bound, pieces=(), kind=jnp.bfloat16):
    drawn = scale * jax.random.normal(stream_key, extent, jnp.float32)
    if pieces:
        drawn = drawn * block_levels(stream_key, extent, pieces, -0.22, 0.18)
    return jnp.clip(drawn, -bound, bound).astype(kind)


def setup_inputs(seed: int = 0) -> dict:
    keys = jax.random.split(jax.random.key(seed), 9)
    clips = draw_clips(jax.random.fold_in(keys[8], 71), 0)
    context = draw_context(jax.random.fold_in(keys[8], 71), 0)
    predict_index = draw_predict_index(jax.random.fold_in(keys[8], 71), 0)
    target_qkv = draw_target_qkv(jax.random.fold_in(keys[8], 71), 0)
    target_out = scatter_about(keys[4], (D, D), D ** -0.5, 0.15625, ((0, 2),))
    student_qkv = draw_student_qkv(jax.random.fold_in(keys[8], 71), 0)
    student_out = scatter_about(keys[6], (D, D), D ** -0.5, 0.15625, ((0, 2), (1, 2)))
    mask_token = draw_mask_token(jax.random.fold_in(keys[8], 71), 0)
    return dict(clips=clips, context=context, predict_index=predict_index, target_qkv=target_qkv, target_out=target_out, student_qkv=student_qkv, student_out=student_out, mask_token=mask_token)


EPSILON = 1e-06
MOMENTUM = 0.99

def layer_norm(values):
    center = values - lax.optimization_barrier(jnp.mean(values, axis=-1, keepdims=True))
    factor = lax.rsqrt(lax.optimization_barrier(jnp.mean(center * center, axis=-1, keepdims=True)) + EPSILON)
    return (center * factor, factor)

def position_table(places, width):
    half_width = width // 2
    spacing = jnp.exp(jnp.arange(half_width, dtype=jnp.float32) * (-math.log(10000.0) / half_width))
    angles = places.astype(jnp.float32)[:, None] * spacing[None, :]
    return jnp.concatenate([jnp.sin(angles), jnp.cos(angles)], axis=1)

def attention(queries, key_rows, value_rows, allowed):
    width = queries.shape[1]
    head_count = width // HEAD_DIM
    query_heads = queries.reshape(queries.shape[0], head_count, HEAD_DIM).transpose(1, 0, 2)
    key_heads = key_rows.reshape(key_rows.shape[0], head_count, HEAD_DIM).transpose(1, 0, 2)
    value_heads = value_rows.reshape(value_rows.shape[0], head_count, HEAD_DIM).transpose(1, 0, 2)
    factor = HEAD_DIM ** (-0.5)

    def one_head(triple):
        query_block, key_block, value_block = triple
        scores = jnp.dot(query_block, key_block.T, preferred_element_type=jnp.float32) * factor
        scores = jnp.where(allowed[None, :], scores, -jnp.inf)
        shifted = jnp.exp(scores - lax.optimization_barrier(jnp.max(scores, axis=1, keepdims=True)))
        mixed = jnp.dot(shifted.astype(jnp.bfloat16), value_block, preferred_element_type=jnp.float32)
        return mixed / lax.optimization_barrier(jnp.sum(shifted, axis=1, keepdims=True))
    outputs = lax.map(one_head, (query_heads, key_heads, value_heads))
    return outputs.transpose(1, 0, 2).reshape(queries.shape[0], width).astype(jnp.bfloat16)

def split_project(mixed, weight):
    part_width = mixed.shape[1] // N_GRP
    result = jnp.zeros((mixed.shape[0], weight.shape[1]), jnp.float32)
    for member in range(N_GRP):
        partial_sum = jnp.dot(mixed[:, member * part_width:(member + 1) * part_width], weight[member * part_width:(member + 1) * part_width], preferred_element_type=jnp.float32)
        result = result + lax.optimization_barrier(partial_sum.astype(jnp.bfloat16)).astype(jnp.float32)
    return result

def clip_gradient(tokens, context, listed, target_qkv, target_out, student_qkv, student_out, mask_token):
    width = tokens.shape[1]
    normed = layer_norm(tokens.astype(jnp.float32))[0].astype(jnp.bfloat16)
    query_t = jnp.dot(normed, target_qkv[0], preferred_element_type=jnp.float32).astype(jnp.bfloat16)
    key_t = jnp.dot(normed, target_qkv[1], preferred_element_type=jnp.float32).astype(jnp.bfloat16)
    value_t = jnp.dot(normed, target_qkv[2], preferred_element_type=jnp.float32).astype(jnp.bfloat16)
    everyone = jnp.ones((tokens.shape[0],), dtype=bool)
    target_mixed = attention(query_t, key_t, value_t, everyone)
    target_sum = split_project(target_mixed, target_out)
    target_features = layer_norm(tokens.astype(jnp.float32) + target_sum)[0].astype(jnp.bfloat16)
    context_keys = jnp.dot(normed, student_qkv[1], preferred_element_type=jnp.float32).astype(jnp.bfloat16)
    context_values = jnp.dot(normed, student_qkv[2], preferred_element_type=jnp.float32).astype(jnp.bfloat16)
    seeds = mask_token[None, :] + position_table(jnp.arange(tokens.shape[0], dtype=jnp.int32), width)
    seed_normed = layer_norm(seeds)[0].astype(jnp.bfloat16)
    seed_queries = jnp.dot(seed_normed, student_qkv[0], preferred_element_type=jnp.float32).astype(jnp.bfloat16)
    student_mixed = attention(seed_queries, context_keys, context_values, context == 1)
    student_sum = split_project(student_mixed, student_out)
    predicted, factor = layer_norm(seeds + student_sum)
    usable = (listed >= 0).astype(jnp.float32)
    counts = jnp.zeros((tokens.shape[0],), jnp.float32).at[jnp.maximum(listed, 0).astype(jnp.int32)].add(usable)
    slope = jnp.clip(predicted - target_features.astype(jnp.float32), -1.0, 1.0) * counts[:, None]
    back_grad = (slope - lax.optimization_barrier(jnp.mean(slope, axis=1, keepdims=True)) - predicted * lax.optimization_barrier(jnp.mean(slope * predicted, axis=1, keepdims=True))) * factor
    return jnp.dot(student_mixed.astype(jnp.float32).T, back_grad, precision=lax.Precision.HIGHEST)

def reference(clips, context, predict_index, target_qkv, target_out, student_qkv, student_out, mask_token):

    def advance(running, inputs):
        tokens, flags, listed = inputs
        return (running + clip_gradient(tokens, flags, listed, target_qkv, target_out, student_qkv, student_out, mask_token), None)
    out_grad, unused = lax.scan(advance, jnp.zeros((D, D), jnp.float32), (clips, context, predict_index))
    target_blend = MOMENTUM * target_out.astype(jnp.float32) + (1.0 - MOMENTUM) * student_out.astype(jnp.float32)
    return (out_grad, target_blend)
```

```python
import math

import jax
import jax.numpy as jnp
from jax import lax
from jax.sharding import PartitionSpec as P

HEAD_DIM = 88
CTX_DEV = 32
EPSILON = 1e-06
MOMENTUM = 0.99
STRIDE = 32


def layer_norm(values):
    center = values - jnp.mean(values, axis=-1, keepdims=True)
    factor = lax.rsqrt(jnp.mean(center * center, axis=-1, keepdims=True) + EPSILON)
    return (center * factor, factor)


def position_table(length, width):
    half_width = width // 2
    spacing = jnp.exp(jnp.arange(half_width, dtype=jnp.float32) * (-math.log(10000.0) / half_width))
    high = (jnp.arange(length // STRIDE) * STRIDE).astype(jnp.float32)[:, None] * spacing[None, :]
    low = jnp.arange(STRIDE).astype(jnp.float32)[:, None] * spacing[None, :]
    sin_h, cos_h = jnp.sin(high), jnp.cos(high)
    sin_l, cos_l = jnp.sin(low), jnp.cos(low)
    first = jnp.concatenate([sin_h, cos_h], axis=1)
    second = jnp.concatenate([cos_h, -sin_h], axis=1)
    twice_c = jnp.concatenate([cos_l, cos_l], axis=1)
    twice_s = jnp.concatenate([sin_l, sin_l], axis=1)
    table = first[:, None, :] * twice_c[None] + second[:, None, :] * twice_s[None]
    return table.reshape(length, width)


def attend(queries, keys, values):
    scores = lax.dot_general(
        queries, keys, (((1,), (1,)), ((), ())), preferred_element_type=jnp.float32
    ) * (HEAD_DIM ** (-0.5))
    shifted = jnp.exp(scores - jnp.max(scores, axis=1, keepdims=True))
    totals = jnp.sum(shifted, axis=1, keepdims=True)
    summed = jnp.dot(shifted.astype(jnp.bfloat16), values, preferred_element_type=jnp.float32)
    return (summed / totals).astype(jnp.bfloat16)


def dot32(left, right):
    return jnp.dot(left, right, preferred_element_type=jnp.float32)


def both_of_dp(block, axis):
    if lax.axis_size("dp") != 2:
        return lax.all_gather(block, "dp", axis=axis, tiled=True)
    other = lax.ppermute(block, "dp", [(0, 1), (1, 0)])
    first = lax.axis_index("dp") == 0
    return jnp.concatenate(
        [jnp.where(first, block, other), jnp.where(first, other, block)], axis=axis
    )


def body(
    clips, context, predict_index, target_qkv, target_out, student_qkv, student_out, mask_token
):
    tokens = clips[0].astype(jnp.float32)
    row_count, width = tokens.shape
    half_width = target_qkv.shape[2]
    head_count = half_width // HEAD_DIM
    shards = lax.axis_size("seq")
    rep = shards // head_count
    length = shards * row_count
    me = lax.axis_index("seq")
    head, part = me // rep, me % rep
    part_rows = length // rep

    def columns(weights):
        return lax.dynamic_slice_in_dim(weights, head * HEAD_DIM, HEAD_DIM, axis=2)

    mine = jnp.concatenate([columns(target_qkv), columns(student_qkv)], axis=0)
    mine = jnp.concatenate([mine[k] for k in range(6)], axis=1)
    weights = both_of_dp(mine, 0)
    relaid = both_of_dp(student_out, 1)

    normed = layer_norm(tokens)[0].astype(jnp.bfloat16)
    every = lax.all_gather(normed, "seq", axis=0, tiled=True)
    small = lax.all_gather(jnp.concatenate([context[0], predict_index[0]]), "seq", axis=0)
    flags, lists = small[:, :row_count], small[:, row_count:].reshape(-1)

    seeds = mask_token[None, :] + position_table(length, width)
    seed_normed = layer_norm(seeds)[0].astype(jnp.bfloat16)

    def own_part(rows):
        if rep == 1:
            return rows
        return lax.dynamic_slice_in_dim(rows, part * part_rows, part_rows, axis=0)

    pick = lambda k: weights[:, k * HEAD_DIM : (k + 1) * HEAD_DIM]
    seed_queries = dot32(own_part(seed_normed), pick(3)).astype(jnp.bfloat16)
    if rep == 1:
        triple = dot32(every, weights[:, : 3 * HEAD_DIM]).astype(jnp.bfloat16)
        query_t = triple[:, :HEAD_DIM]
        pair_t = triple[:, HEAD_DIM:]
    else:
        query_t = dot32(own_part(every), pick(0)).astype(jnp.bfloat16)
        pair_t = dot32(every, weights[:, HEAD_DIM : 3 * HEAD_DIM]).astype(jnp.bfloat16)
    target_mixed = attend(query_t, pair_t[:, :HEAD_DIM], pair_t[:, HEAD_DIM:])

    is_context = flags == 1
    order = jnp.cumsum(is_context.astype(jnp.int32), axis=1) - 1
    selector = (
        (order[:, None, :] == jnp.arange(CTX_DEV, dtype=jnp.int32)[None, :, None])
        & is_context[:, None, :]
    ).astype(jnp.bfloat16)
    chosen = jnp.einsum(
        "sck,skw->scw",
        selector,
        every.reshape(shards, row_count, width),
        preferred_element_type=jnp.float32,
    ).astype(jnp.bfloat16)
    chosen = chosen.reshape(shards * CTX_DEV, width)
    pair_s = dot32(chosen, weights[:, 4 * HEAD_DIM :]).astype(jnp.bfloat16)
    student_mixed = attend(seed_queries, pair_s[:, :HEAD_DIM], pair_s[:, HEAD_DIM:])

    both = jnp.concatenate([target_mixed, student_mixed], axis=1)
    if rep == 1:
        both = both.reshape(shards, row_count, 2 * HEAD_DIM)
        both = lax.all_to_all(both, "seq", split_axis=0, concat_axis=0, tiled=True)
    else:
        both = lax.all_gather(both, "seq", axis=0, tiled=True)
        both = both.reshape(head_count, length, 2 * HEAD_DIM)
        both = lax.dynamic_slice_in_dim(both, me * row_count, row_count, axis=1)
    own_target = both[:, :, :HEAD_DIM].transpose(1, 0, 2).reshape(row_count, half_width)
    own_student = both[:, :, HEAD_DIM:].transpose(1, 0, 2).reshape(row_count, half_width)
    sums = jnp.concatenate(
        [
            dot32(own_target, target_out).astype(jnp.bfloat16),
            dot32(own_student, relaid).astype(jnp.bfloat16),
        ],
        axis=0,
    )
    if lax.axis_size("grp") == 2:
        other = lax.ppermute(sums, "grp", [(0, 1), (1, 0)])
        sums = sums.astype(jnp.float32) + other.astype(jnp.float32)
    else:
        sums = lax.psum(sums, "grp").astype(jnp.float32)

    features = layer_norm(tokens + sums[:row_count])[0].astype(jnp.bfloat16)
    own_seeds = lax.dynamic_slice_in_dim(seeds, me * row_count, row_count, axis=0)
    predicted, factor = layer_norm(own_seeds + sums[row_count:])
    places = me * row_count + jnp.arange(row_count, dtype=jnp.int32)
    usable = jnp.sum((lists[None, :] == places[:, None]).astype(jnp.float32), axis=1)
    slope = jnp.clip(predicted - features.astype(jnp.float32), -1.0, 1.0) * usable[:, None]
    back_grad = (
        slope
        - jnp.mean(slope, axis=1, keepdims=True)
        - predicted * jnp.mean(slope * predicted, axis=1, keepdims=True)
    ) * factor
    back_all = lax.all_gather(back_grad.astype(jnp.bfloat16), "seq", axis=0, tiled=True)
    head_grad = lax.dot_general(
        student_mixed,
        own_part(back_all),
        (((0,), (0,)), ((), ())),
        preferred_element_type=jnp.float32,
    ).astype(jnp.bfloat16)
    if lax.axis_size("dp") == 2:
        half = head_grad.shape[1] // 2
        first = lax.axis_index("dp") == 0
        low, high = head_grad[:, :half], head_grad[:, half:]
        keep, send = jnp.where(first, low, high), jnp.where(first, high, low)
        came = lax.ppermute(send, "dp", [(0, 1), (1, 0)])
        head_grad = (keep.astype(jnp.float32) + came.astype(jnp.float32)).astype(jnp.bfloat16)
    else:
        head_grad = lax.psum_scatter(head_grad, "dp", scatter_dimension=1, tiled=True)
    out_grad = lax.all_gather(head_grad, "seq", axis=0, tiled=True).astype(jnp.float32)
    if rep > 1:
        out_grad = out_grad.reshape(head_count, rep, HEAD_DIM, -1).sum(1)
        out_grad = out_grad.reshape(half_width, -1)
    target_blend = MOMENTUM * target_out.astype(jnp.float32) + (1.0 - MOMENTUM) * relaid.astype(
        jnp.float32
    )
    return (out_grad, target_blend)


def solution(mesh):
    in_specs = (
        P("dp", "seq", None),
        P("dp", "seq"),
        P("dp", "seq"),
        P(None, "dp", "grp"),
        P("grp", None),
        P(None, "dp", "grp"),
        P("grp", "dp"),
        P(),
    )
    out_specs = (P("grp", "dp"), P("grp", None))
    return jax.shard_map(body, mesh=mesh, in_specs=in_specs, out_specs=out_specs, check_vma=False)
```

```python
import functools
import math

import jax
import jax.numpy as jnp
from jax import lax
from jax.experimental import pallas as pl
from jax.experimental.pallas import tpu as pltpu
from jax.sharding import PartitionSpec as P

MESH = pl.DeviceIdType.MESH
CHUNKS = 2

HEAD_DIM = 88
CTX_DEV = 32
EPSILON = 1e-06
MOMENTUM = 0.99
STRIDE = 32


def layer_norm(values):
    center = values - jnp.mean(values, axis=-1, keepdims=True)
    factor = lax.rsqrt(jnp.mean(center * center, axis=-1, keepdims=True) + EPSILON)
    return (center * factor, factor)


def position_tables(length, width):
    half_width = width // 2
    spacing = jnp.exp(jnp.arange(half_width, dtype=jnp.float32) * (-math.log(10000.0) / half_width))
    high = (jnp.arange(length // STRIDE) * STRIDE).astype(jnp.float32)[:, None] * spacing[None, :]
    low = jnp.arange(STRIDE).astype(jnp.float32)[:, None] * spacing[None, :]
    sin_h, cos_h = jnp.sin(high), jnp.cos(high)
    sin_l, cos_l = jnp.sin(low), jnp.cos(low)
    return (
        jnp.concatenate([sin_h, cos_h], axis=1),
        jnp.concatenate([cos_h, -sin_h], axis=1),
        jnp.concatenate([cos_l, cos_l], axis=1),
        jnp.concatenate([sin_l, sin_l], axis=1),
    )


def norm_seed_block(index, tables, mask_ref, seed_out):
    first, second, twice_c, twice_s = tables
    rows = pl.ds(index, 1)
    seeds = mask_ref[...] + (first[rows, :] * twice_c[...] + second[rows, :] * twice_s[...])
    start = pl.multiple_of(index * STRIDE, STRIDE)
    seed_out[pl.ds(start, STRIDE), :] = layer_norm(seeds)[0].astype(jnp.bfloat16)


def gather_kernel(shards, with_seeds, *refs):
    if with_seeds:
        (x_ref, small_ref, *tables, mask_ref, out_ref, small_out, seed_out) = refs[:10]
        sems = refs[10:]
        s_send, s_recv, s_own = sems[7:]
    else:
        x_ref, out_ref = refs[:2]
        sems = refs[2:]
    own_sem, z_send, z_recv, m_send, m_recv, y_send, y_recv = sems[:7]
    me, grp = lax.axis_index("seq"), lax.axis_index("grp")
    z, core = me // 2, me % 2
    depth = shards // 2
    mate, across = z * 2 + (1 - core), 1 - grp
    pieces = range(CHUNKS)

    barrier = pltpu.get_barrier_semaphore()
    if with_seeds:
        for k in range(1, shards):
            peer = {"seq": lax.rem(me + k, shards)}
            pl.semaphore_signal(barrier, inc=1, device_id=peer, device_id_type=MESH)
        greeted = shards - 1
    else:
        for k in range(1, depth):
            peer = {"seq": lax.rem(z + k, depth) * 2 + core}
            pl.semaphore_signal(barrier, inc=1, device_id=peer, device_id_type=MESH)
        pl.semaphore_signal(barrier, inc=1, device_id={"seq": mate}, device_id_type=MESH)
        greeted = depth
    pl.semaphore_signal(barrier, inc=1, device_id={"grp": across}, device_id_type=MESH)
    pl.semaphore_wait(barrier, greeted + 1)

    def remote(src, slot, group, piece, send, recv, to):
        return pltpu.make_async_remote_copy(
            src_ref=src,
            dst_ref=out_ref.at[slot, group, piece],
            send_sem=send,
            recv_sem=recv,
            device_id=to,
            device_id_type=MESH,
        )

    def z_copy(way, dist, piece):
        sign = 1 - 2 * way
        to = {"seq": (z + sign * dist) * 2 + core}
        return remote(
            x_ref.at[piece], me, grp, piece,
            z_send.at[way, dist - 1, piece], z_recv.at[way, dist - 1, piece], to,
        )

    def goes(way, dist):
        return z + dist < depth if way == 0 else z - dist >= 0

    def comes(way, dist):
        return goes(1 - way, dist)

    def mate_copy(src, source, side, piece):
        group = grp if side == 0 else across
        return remote(
            src, source * 2 + core, group, piece,
            m_send.at[side, source, piece], m_recv.at[side, source, piece], {"seq": mate},
        )

    def y_copy(src, source, piece):
        return remote(
            src, source * 2 + core, grp, piece,
            y_send.at[source, piece], y_recv.at[source, piece], {"grp": across},
        )

    def small_copy(k):
        return pltpu.make_async_remote_copy(
            src_ref=small_ref,
            dst_ref=small_out.at[me],
            send_sem=s_send.at[k - 1],
            recv_sem=s_recv.at[k - 1],
            device_id={"seq": lax.rem(me + k, shards)},
            device_id_type=MESH,
        )

    for dist in range(1, depth):
        for way in range(2):

            @pl.when(goes(way, dist))
            def _():
                for piece in pieces:
                    z_copy(way, dist, piece).start()

    for piece in pieces:
        y_copy(x_ref.at[piece], z, piece).start()
        mate_copy(x_ref.at[piece], z, 0, piece).start()
    own = pltpu.make_async_copy(x_ref, out_ref.at[me, grp], own_sem)
    own.start()
    if with_seeds:
        for k in range(1, shards):
            small_copy(k).start()
        small_own = pltpu.make_async_copy(small_ref, small_out.at[me], s_own)
        small_own.start()
        blocks = seed_out.shape[0] // STRIDE
        stages = depth + 1

    def work(stage):
        if with_seeds:
            lax.fori_loop(
                stage * blocks // stages,
                (stage + 1) * blocks // stages,
                lambda i, _: (norm_seed_block(i, tables, mask_ref, seed_out), 0)[1],
                0,
            )

    def from_z(way, dist):
        source = z - dist if way == 0 else z + dist

        @pl.when(comes(way, dist))
        def _():
            for piece in pieces:
                z_copy(way, dist, piece).wait_recv()
                held = out_ref.at[source * 2 + core, grp, piece]
                y_copy(held, source, piece).start()
                mate_copy(held, source, 0, piece).start()

    def from_y(source):
        for piece in pieces:
            held = out_ref.at[source * 2 + core, across, piece]
            y_copy(held, source, piece).wait_recv()
            mate_copy(held, source, 1, piece).start()

    work(0)
    from_y(z)
    for dist in range(1, depth):
        work(dist)
        for way in range(2):
            from_z(way, dist)
        if dist > 1:
            for way in range(2):

                @pl.when(comes(way, dist - 1))
                def _():
                    from_y(z - (dist - 1) if way == 0 else z + (dist - 1))

    work(depth)
    for way in range(2):

        @pl.when(comes(way, depth - 1))
        def _():
            from_y(z - (depth - 1) if way == 0 else z + (depth - 1))

    for source in range(depth):
        for piece in pieces:
            for side in range(2):
                mate_copy(out_ref.at[source * 2 + core, grp, piece], source, side, piece).wait()
            y_copy(out_ref.at[source * 2 + core, grp, piece], source, piece).wait_send()
    for dist in range(1, depth):
        for way in range(2):

            @pl.when(goes(way, dist))
            def _():
                for piece in pieces:
                    z_copy(way, dist, piece).wait_send()

    own.wait()
    if with_seeds:
        for k in range(1, shards):
            small_copy(k).wait()
        small_own.wait()


def gather_rows(rows, shards, small=None, tables=None, mask=None):
    count, width = rows.shape
    depth = shards // 2
    dma = pltpu.SemaphoreType.DMA
    shaped = rows.reshape(CHUNKS, count // CHUNKS, width)
    out_shape = [jax.ShapeDtypeStruct((shards, 2) + shaped.shape, rows.dtype)]
    operands = [shaped]
    scratch = [
        dma,
        dma((2, depth - 1, CHUNKS)),
        dma((2, depth - 1, CHUNKS)),
        dma((2, depth, CHUNKS)),
        dma((2, depth, CHUNKS)),
        dma((depth, CHUNKS)),
        dma((depth, CHUNKS)),
    ]
    with_seeds = small is not None
    if with_seeds:
        operands += [small, *tables, mask[None, :]]
        out_shape += [
            jax.ShapeDtypeStruct((shards,) + small.shape, small.dtype),
            jax.ShapeDtypeStruct((tables[0].shape[0] * STRIDE, width), jnp.bfloat16),
        ]
        scratch += [dma((shards - 1,)), dma((shards - 1,)), dma]
    vmem = pl.BlockSpec(memory_space=pltpu.VMEM)
    results = pl.pallas_call(
        functools.partial(gather_kernel, shards, with_seeds),
        out_shape=out_shape,
        in_specs=[vmem] * len(operands),
        out_specs=[vmem] * len(out_shape),
        scratch_shapes=scratch,
        name="gather_seeds" if with_seeds else "gather_rows",
        compiler_params=pltpu.CompilerParams(
            collective_id=1 if with_seeds else 2,
            has_side_effects=True,
            vmem_limit_bytes=48 * 1024 * 1024,
        ),
    )(*operands)
    return (results[0].reshape(shards * 2 * count, width), *results[1:])


def attend(queries, keys, values):
    scores = lax.dot_general(
        queries, keys, (((1,), (1,)), ((), ())), preferred_element_type=jnp.float32
    ) * (HEAD_DIM ** (-0.5))
    shifted = jnp.exp(scores - jnp.max(scores, axis=1, keepdims=True))
    totals = jnp.sum(shifted, axis=1, keepdims=True)
    summed = jnp.dot(shifted.astype(jnp.bfloat16), values, preferred_element_type=jnp.float32)
    return (summed / totals).astype(jnp.bfloat16)


def dot32(left, right):
    return jnp.dot(left, right, preferred_element_type=jnp.float32)


def both_of_dp(block, axis):
    if lax.axis_size("dp") != 2:
        return lax.all_gather(block, "dp", axis=axis, tiled=True)
    other = lax.ppermute(block, "dp", [(0, 1), (1, 0)])
    first = lax.axis_index("dp") == 0
    return jnp.concatenate(
        [jnp.where(first, block, other), jnp.where(first, other, block)], axis=axis
    )


def body(
    clips, context, predict_index, target_qkv, target_out, student_qkv, student_out, mask_token
):
    row_count, width = clips.shape[1:]
    half_width = target_qkv.shape[2]
    head_count = half_width // HEAD_DIM
    shards = lax.axis_size("seq")
    rep = shards // head_count
    length = shards * row_count
    me = lax.axis_index("seq")
    head, part = me // rep, me % rep
    part_rows = length // rep

    def columns(weights):
        return lax.dynamic_slice_in_dim(weights, head * HEAD_DIM, HEAD_DIM, axis=2)

    mine = jnp.concatenate([columns(target_qkv), columns(student_qkv)], axis=0)
    mine = jnp.concatenate([mine[k] for k in range(6)], axis=1)
    weights = both_of_dp(mine, 0)
    relaid = both_of_dp(student_out, 1)

    grp = lax.axis_index("grp")
    half_rows = row_count // 2
    own_tokens = lax.dynamic_slice_in_dim(clips[0], grp * half_rows, half_rows, axis=0)
    own_tokens = own_tokens.astype(jnp.float32)
    normed = layer_norm(own_tokens)[0].astype(jnp.bfloat16)
    tables = position_tables(length, width)
    small = jnp.concatenate([context[0], predict_index[0]])[None, :]
    small = jnp.pad(small, ((0, 7), (0, -small.shape[1] % 128)))
    every, small, seed_normed = gather_rows(normed, shards, small, tables, mask_token)
    small = small[:, 0]
    flags = small[:, :row_count]
    lists = small[:, row_count : row_count + predict_index.shape[1]].reshape(-1)

    def own_part(rows):
        if rep == 1:
            return rows
        return lax.dynamic_slice_in_dim(rows, part * part_rows, part_rows, axis=0)

    pick = lambda k: weights[:, k * HEAD_DIM : (k + 1) * HEAD_DIM]
    seed_queries = dot32(own_part(seed_normed), pick(3)).astype(jnp.bfloat16)
    if rep == 1:
        triple = dot32(every, weights[:, : 3 * HEAD_DIM]).astype(jnp.bfloat16)
        query_t = triple[:, :HEAD_DIM]
        pair_t = triple[:, HEAD_DIM:]
    else:
        query_t = dot32(own_part(every), pick(0)).astype(jnp.bfloat16)
        pair_t = dot32(every, weights[:, HEAD_DIM : 3 * HEAD_DIM]).astype(jnp.bfloat16)
    target_mixed = attend(query_t, pair_t[:, :HEAD_DIM], pair_t[:, HEAD_DIM:])

    is_context = flags == 1
    order = jnp.cumsum(is_context.astype(jnp.int32), axis=1) - 1
    selector = (
        (order[:, None, :] == jnp.arange(CTX_DEV, dtype=jnp.int32)[None, :, None])
        & is_context[:, None, :]
    ).astype(jnp.bfloat16)
    chosen = jnp.einsum(
        "sck,skw->scw",
        selector,
        every.reshape(shards, row_count, width),
        preferred_element_type=jnp.float32,
    ).astype(jnp.bfloat16)
    chosen = chosen.reshape(shards * CTX_DEV, width)
    pair_s = dot32(chosen, weights[:, 4 * HEAD_DIM :]).astype(jnp.bfloat16)
    student_mixed = attend(seed_queries, pair_s[:, :HEAD_DIM], pair_s[:, HEAD_DIM:])

    both = jnp.concatenate([target_mixed, student_mixed], axis=1)
    if rep == 1:
        both = both.reshape(shards, row_count, 2 * HEAD_DIM)
        both = lax.all_to_all(both, "seq", split_axis=0, concat_axis=0, tiled=True)
    else:
        both = lax.all_gather(both, "seq", axis=0, tiled=True)
        both = both.reshape(head_count, length, 2 * HEAD_DIM)
        both = lax.dynamic_slice_in_dim(both, me * row_count, row_count, axis=1)
    own_target = both[:, :, :HEAD_DIM].transpose(1, 0, 2).reshape(row_count, half_width)
    own_student = both[:, :, HEAD_DIM:].transpose(1, 0, 2).reshape(row_count, half_width)
    sums = jnp.stack(
        [
            dot32(own_target, target_out).astype(jnp.bfloat16),
            dot32(own_student, relaid).astype(jnp.bfloat16),
        ]
    )
    low, high = sums[:, :half_rows], sums[:, half_rows:]
    keep, send = jnp.where(grp == 0, low, high), jnp.where(grp == 0, high, low)
    came = lax.ppermute(send, "grp", [(0, 1), (1, 0)])
    sums = keep.astype(jnp.float32) + came.astype(jnp.float32)

    features = layer_norm(own_tokens + sums[0])[0].astype(jnp.bfloat16)
    base = me * row_count + grp * half_rows
    first, second, twice_c, twice_s = tables
    blocks = half_rows // STRIDE
    first = lax.dynamic_slice_in_dim(first, base // STRIDE, blocks, axis=0)
    second = lax.dynamic_slice_in_dim(second, base // STRIDE, blocks, axis=0)
    own_seeds = first[:, None] * twice_c[None] + second[:, None] * twice_s[None]
    own_seeds = mask_token[None, :] + own_seeds.reshape(half_rows, width)
    predicted, factor = layer_norm(own_seeds + sums[1])
    places = base + jnp.arange(half_rows, dtype=jnp.int32)
    usable = jnp.sum((lists[None, :] == places[:, None]).astype(jnp.float32), axis=1)
    slope = jnp.clip(predicted - features.astype(jnp.float32), -1.0, 1.0) * usable[:, None]
    back_grad = (
        slope
        - jnp.mean(slope, axis=1, keepdims=True)
        - predicted * jnp.mean(slope * predicted, axis=1, keepdims=True)
    ) * factor
    back_all = gather_rows(back_grad.astype(jnp.bfloat16), shards)[0]
    head_grad = lax.dot_general(
        student_mixed,
        own_part(back_all),
        (((0,), (0,)), ((), ())),
        preferred_element_type=jnp.float32,
    ).astype(jnp.bfloat16)
    if lax.axis_size("dp") == 2:
        half = head_grad.shape[1] // 2
        first = lax.axis_index("dp") == 0
        low, high = head_grad[:, :half], head_grad[:, half:]
        keep, send = jnp.where(first, low, high), jnp.where(first, high, low)
        came = lax.ppermute(send, "dp", [(0, 1), (1, 0)])
        head_grad = (keep.astype(jnp.float32) + came.astype(jnp.float32)).astype(jnp.bfloat16)
    else:
        head_grad = lax.psum_scatter(head_grad, "dp", scatter_dimension=1, tiled=True)
    out_grad = lax.all_gather(head_grad, "seq", axis=0, tiled=True).astype(jnp.float32)
    if rep > 1:
        out_grad = out_grad.reshape(head_count, rep, HEAD_DIM, -1).sum(1)
        out_grad = out_grad.reshape(half_width, -1)
    target_blend = MOMENTUM * target_out.astype(jnp.float32) + (1.0 - MOMENTUM) * relaid.astype(
        jnp.float32
    )
    return (out_grad, target_blend)


def solution(mesh):
    in_specs = (
        P("dp", "seq", None),
        P("dp", "seq"),
        P("dp", "seq"),
        P(None, "dp", "grp"),
        P("grp", None),
        P(None, "dp", "grp"),
        P("grp", "dp"),
        P(),
    )
    out_specs = (P("grp", "dp"), P("grp", None))
    return jax.shard_map(body, mesh=mesh, in_specs=in_specs, out_specs=out_specs, check_vma=False)
```

```python
import functools
import math

import jax
import jax.numpy as jnp
from jax import lax
from jax.experimental import pallas as pl
from jax.experimental.pallas import tpu as pltpu
from jax.sharding import PartitionSpec as P

MESH = pl.DeviceIdType.MESH
CHUNKS = 2

HEAD_DIM = 88
CTX_DEV = 32
EPSILON = 1e-06
MOMENTUM = 0.99
STRIDE = 32


def layer_norm(values):
    center = values - jnp.mean(values, axis=-1, keepdims=True)
    factor = lax.rsqrt(jnp.mean(center * center, axis=-1, keepdims=True) + EPSILON)
    return (center * factor, factor)


def position_tables(length, width):
    half_width = width // 2
    spacing = jnp.exp(jnp.arange(half_width, dtype=jnp.float32) * (-math.log(10000.0) / half_width))
    high = (jnp.arange(length // STRIDE) * STRIDE).astype(jnp.float32)[:, None] * spacing[None, :]
    low = jnp.arange(STRIDE).astype(jnp.float32)[:, None] * spacing[None, :]
    sin_h, cos_h = jnp.sin(high), jnp.cos(high)
    sin_l, cos_l = jnp.sin(low), jnp.cos(low)
    return (
        jnp.concatenate([sin_h, cos_h], axis=1),
        jnp.concatenate([cos_h, -sin_h], axis=1),
        jnp.concatenate([cos_l, cos_l], axis=1),
        jnp.concatenate([sin_l, sin_l], axis=1),
    )


def norm_seed_block(index, tables, mask_ref, seed_out):
    first, second, twice_c, twice_s = tables
    rows = pl.ds(index, 1)
    seeds = mask_ref[...] + (first[rows, :] * twice_c[...] + second[rows, :] * twice_s[...])
    start = pl.multiple_of(index * STRIDE, STRIDE)
    seed_out[pl.ds(start, STRIDE), :] = layer_norm(seeds)[0].astype(jnp.bfloat16)


def gather_kernel(shards, with_seeds, *refs):
    if with_seeds:
        (x_ref, small_ref, *tables, mask_ref, out_ref, small_out, seed_out) = refs[:10]
        sems = refs[10:]
        s_send, s_recv, s_own = sems[7:]
    else:
        x_ref, out_ref = refs[:2]
        sems = refs[2:]
    own_sem, z_send, z_recv, m_send, m_recv, y_send, y_recv = sems[:7]
    me, grp = lax.axis_index("seq"), lax.axis_index("grp")
    z, core = me // 2, me % 2
    depth = shards // 2
    mate, across = z * 2 + (1 - core), 1 - grp
    pieces = range(CHUNKS)

    barrier = pltpu.get_barrier_semaphore()
    if with_seeds:
        for k in range(1, shards):
            peer = {"seq": lax.rem(me + k, shards)}
            pl.semaphore_signal(barrier, inc=1, device_id=peer, device_id_type=MESH)
        greeted = shards - 1
    else:
        for k in range(1, depth):
            peer = {"seq": lax.rem(z + k, depth) * 2 + core}
            pl.semaphore_signal(barrier, inc=1, device_id=peer, device_id_type=MESH)
        pl.semaphore_signal(barrier, inc=1, device_id={"seq": mate}, device_id_type=MESH)
        greeted = depth
    pl.semaphore_signal(barrier, inc=1, device_id={"grp": across}, device_id_type=MESH)
    pl.semaphore_wait(barrier, greeted + 1)

    def remote(src, slot, group, piece, send, recv, to):
        return pltpu.make_async_remote_copy(
            src_ref=src,
            dst_ref=out_ref.at[slot, group, piece],
            send_sem=send,
            recv_sem=recv,
            device_id=to,
            device_id_type=MESH,
        )

    def z_copy(way, dist, piece):
        sign = 1 - 2 * way
        to = {"seq": (z + sign * dist) * 2 + core}
        return remote(
            x_ref.at[piece], me, grp, piece,
            z_send.at[way, dist - 1, piece], z_recv.at[way, dist - 1, piece], to,
        )

    def goes(way, dist):
        return z + dist < depth if way == 0 else z - dist >= 0

    def comes(way, dist):
        return goes(1 - way, dist)

    def mate_copy(src, source, side, piece):
        group = grp if side == 0 else across
        return remote(
            src, source * 2 + core, group, piece,
            m_send.at[side, source, piece], m_recv.at[side, source, piece], {"seq": mate},
        )

    def y_copy(src, source, piece):
        return remote(
            src, source * 2 + core, grp, piece,
            y_send.at[source, piece], y_recv.at[source, piece], {"grp": across},
        )

    def small_copy(k):
        return pltpu.make_async_remote_copy(
            src_ref=small_ref,
            dst_ref=small_out.at[me],
            send_sem=s_send.at[k - 1],
            recv_sem=s_recv.at[k - 1],
            device_id={"seq": lax.rem(me + k, shards)},
            device_id_type=MESH,
        )

    for dist in range(1, depth):
        for way in range(2):

            @pl.when(goes(way, dist))
            def _():
                for piece in pieces:
                    z_copy(way, dist, piece).start()

    for piece in pieces:
        y_copy(x_ref.at[piece], z, piece).start()
        mate_copy(x_ref.at[piece], z, 0, piece).start()
    own = pltpu.make_async_copy(x_ref, out_ref.at[me, grp], own_sem)
    own.start()
    if with_seeds:
        for k in range(1, shards):
            small_copy(k).start()
        small_own = pltpu.make_async_copy(small_ref, small_out.at[me], s_own)
        small_own.start()
        blocks = seed_out.shape[0] // STRIDE
        stages = depth + 1

    def work(stage):
        if with_seeds:
            lax.fori_loop(
                stage * blocks // stages,
                (stage + 1) * blocks // stages,
                lambda i, _: (norm_seed_block(i, tables, mask_ref, seed_out), 0)[1],
                0,
            )

    def from_z(way, dist):
        source = z - dist if way == 0 else z + dist

        @pl.when(comes(way, dist))
        def _():
            for piece in pieces:
                z_copy(way, dist, piece).wait_recv()
                held = out_ref.at[source * 2 + core, grp, piece]
                y_copy(held, source, piece).start()
                mate_copy(held, source, 0, piece).start()

    def from_y(source):
        for piece in pieces:
            held = out_ref.at[source * 2 + core, across, piece]
            y_copy(held, source, piece).wait_recv()
            mate_copy(held, source, 1, piece).start()

    work(0)
    from_y(z)
    for dist in range(1, depth):
        work(dist)
        for way in range(2):
            from_z(way, dist)
        if dist > 1:
            for way in range(2):

                @pl.when(comes(way, dist - 1))
                def _():
                    from_y(z - (dist - 1) if way == 0 else z + (dist - 1))

    work(depth)
    for way in range(2):

        @pl.when(comes(way, depth - 1))
        def _():
            from_y(z - (depth - 1) if way == 0 else z + (depth - 1))

    for source in range(depth):
        for piece in pieces:
            for side in range(2):
                mate_copy(out_ref.at[source * 2 + core, grp, piece], source, side, piece).wait()
            y_copy(out_ref.at[source * 2 + core, grp, piece], source, piece).wait_send()
    for dist in range(1, depth):
        for way in range(2):

            @pl.when(goes(way, dist))
            def _():
                for piece in pieces:
                    z_copy(way, dist, piece).wait_send()

    own.wait()
    if with_seeds:
        for k in range(1, shards):
            small_copy(k).wait()
        small_own.wait()


def gather_rows(rows, shards, small=None, tables=None, mask=None):
    count, width = rows.shape
    depth = shards // 2
    dma = pltpu.SemaphoreType.DMA
    shaped = rows.reshape(CHUNKS, count // CHUNKS, width)
    out_shape = [jax.ShapeDtypeStruct((shards, 2) + shaped.shape, rows.dtype)]
    operands = [shaped]
    scratch = [
        dma,
        dma((2, depth - 1, CHUNKS)),
        dma((2, depth - 1, CHUNKS)),
        dma((2, depth, CHUNKS)),
        dma((2, depth, CHUNKS)),
        dma((depth, CHUNKS)),
        dma((depth, CHUNKS)),
    ]
    with_seeds = small is not None
    if with_seeds:
        operands += [small, *tables, mask[None, :]]
        out_shape += [
            jax.ShapeDtypeStruct((shards,) + small.shape, small.dtype),
            jax.ShapeDtypeStruct((tables[0].shape[0] * STRIDE, width), jnp.bfloat16),
        ]
        scratch += [dma((shards - 1,)), dma((shards - 1,)), dma]
    vmem = pl.BlockSpec(memory_space=pltpu.VMEM)
    results = pl.pallas_call(
        functools.partial(gather_kernel, shards, with_seeds),
        out_shape=out_shape,
        in_specs=[vmem] * len(operands),
        out_specs=[vmem] * len(out_shape),
        scratch_shapes=scratch,
        name="gather_seeds" if with_seeds else "gather_rows",
        compiler_params=pltpu.CompilerParams(
            collective_id=1 if with_seeds else 2,
            has_side_effects=True,
            vmem_limit_bytes=48 * 1024 * 1024,
        ),
    )(*operands)
    return (results[0].reshape(shards * 2 * count, width), *results[1:])


def middle_kernel(shards, *refs):
    (
        q_t, k_t, v_t, q_s, k_s, v_s, out_t, out_s, tokens_ref, seeds_ref, usable_ref,
        back_ref, mix_s, mix_t, got_t, got_s, part_t, part_s, came_t, came_s,
        send_t, recv_t, send_s, recv_s, y_send, y_recv,
    ) = refs
    me, grp = lax.axis_index("seq"), lax.axis_index("grp")
    across = 1 - grp

    barrier = pltpu.get_barrier_semaphore()
    for k in range(1, shards):
        peer = {"seq": lax.rem(me + k, shards)}
        pl.semaphore_signal(barrier, inc=1, device_id=peer, device_id_type=MESH)
    pl.semaphore_signal(barrier, inc=1, device_id={"grp": across}, device_id_type=MESH)
    pl.semaphore_wait(barrier, shards)

    def turn(k):
        return lax.rem(me + 1 + k, shards)

    def copy(k, mix, got, send, recv):
        return pltpu.make_async_remote_copy(
            src_ref=mix.at[turn(k)],
            dst_ref=got.at[me],
            send_sem=send.at[k],
            recv_sem=recv.at[k],
            device_id={"seq": turn(k)},
            device_id_type=MESH,
        )

    def heads(queries, keys, values, mix, got, send, recv):
        def step(k, carry):
            dest = turn(k)
            mix[dest] = attend(queries[dest], keys[...], values[...])

            @pl.when(k > 0)
            def _():
                copy(k - 1, mix, got, send, recv).start()

            return carry

        lax.fori_loop(0, shards, step, 0)
        got[me] = mix[me]

    def y_copy(index, part, came):
        return pltpu.make_async_remote_copy(
            src_ref=part.at[across],
            dst_ref=came,
            send_sem=y_send.at[index],
            recv_sem=y_recv.at[index],
            device_id={"grp": across},
            device_id_type=MESH,
        )

    def project(got, weights, part):
        rows = jnp.concatenate([got[k] for k in range(shards)], axis=1)
        whole = dot32(rows, weights[...]).astype(jnp.bfloat16)
        half = whole.shape[0] // 2
        part[0] = whole[:half]
        part[1] = whole[half:]

    def total(part, came):
        return part[grp].astype(jnp.float32) + came[...].astype(jnp.float32)

    heads(q_t, k_t, v_t, mix_t, got_t, send_t, recv_t)
    heads(q_s, k_s, v_s, mix_s, got_s, send_s, recv_s)
    for k in range(shards - 1):
        copy(k, mix_t, got_t, send_t, recv_t).wait_recv()
    project(got_t, out_t, part_t)
    copy(0, mix_s, got_s, send_s, recv_s).wait_recv()
    y_copy(0, part_t, came_t).start()
    for k in range(1, shards - 1):
        copy(k, mix_s, got_s, send_s, recv_s).wait_recv()
    project(got_s, out_s, part_s)
    y_copy(0, part_t, came_t).wait_recv()
    y_copy(1, part_s, came_s).start()
    tokens = tokens_ref[...].astype(jnp.float32)
    features = layer_norm(tokens + total(part_t, came_t))[0].astype(jnp.bfloat16)
    y_copy(1, part_s, came_s).wait_recv()
    predicted, factor = layer_norm(seeds_ref[...] + total(part_s, came_s))
    back_ref[...] = gradient(predicted, factor, features, usable_ref[...]).astype(jnp.bfloat16)
    for k in range(shards - 1):
        copy(k, mix_t, got_t, send_t, recv_t).wait_send()
        copy(k, mix_s, got_s, send_s, recv_s).wait_send()
    y_copy(0, part_t, came_t).wait_send()
    y_copy(1, part_s, came_s).wait_send()


def middle(shards, operands):
    q_t = operands[0]
    rows, width = operands[8].shape
    bf16, dma = jnp.bfloat16, pltpu.SemaphoreType.DMA
    vmem = pl.BlockSpec(memory_space=pltpu.VMEM)
    return pl.pallas_call(
        functools.partial(middle_kernel, shards),
        out_shape=[
            jax.ShapeDtypeStruct((rows, width), bf16),
            jax.ShapeDtypeStruct(q_t.shape, bf16),
        ],
        in_specs=[vmem] * len(operands),
        out_specs=[vmem] * 2,
        scratch_shapes=[pltpu.VMEM(q_t.shape, bf16)] * 3
        + [pltpu.VMEM((2, rows, width), bf16)] * 2
        + [pltpu.VMEM((rows, width), bf16)] * 2
        + [dma((shards - 1,))] * 4
        + [dma((2,))] * 2,
        name="middle",
        compiler_params=pltpu.CompilerParams(
            collective_id=3, has_side_effects=True, vmem_limit_bytes=48 * 1024 * 1024
        ),
    )(*operands)


def gradient(predicted, factor, features, usable):
    slope = jnp.clip(predicted - features.astype(jnp.float32), -1.0, 1.0) * usable
    return (
        slope
        - jnp.mean(slope, axis=1, keepdims=True)
        - predicted * jnp.mean(slope * predicted, axis=1, keepdims=True)
    ) * factor


def attend(queries, keys, values):
    scores = lax.dot_general(
        queries, keys, (((1,), (1,)), ((), ())), preferred_element_type=jnp.float32
    ) * (HEAD_DIM ** (-0.5))
    shifted = jnp.exp(scores - jnp.max(scores, axis=1, keepdims=True))
    totals = jnp.sum(shifted, axis=1, keepdims=True)
    summed = jnp.dot(shifted.astype(jnp.bfloat16), values, preferred_element_type=jnp.float32)
    return (summed / totals).astype(jnp.bfloat16)


def dot32(left, right):
    return jnp.dot(left, right, preferred_element_type=jnp.float32)


def both_of_dp(block, axis):
    if lax.axis_size("dp") != 2:
        return lax.all_gather(block, "dp", axis=axis, tiled=True)
    other = lax.ppermute(block, "dp", [(0, 1), (1, 0)])
    first = lax.axis_index("dp") == 0
    return jnp.concatenate(
        [jnp.where(first, block, other), jnp.where(first, other, block)], axis=axis
    )


def body(
    clips, context, predict_index, target_qkv, target_out, student_qkv, student_out, mask_token
):
    row_count, width = clips.shape[1:]
    half_width = target_qkv.shape[2]
    head_count = half_width // HEAD_DIM
    shards = lax.axis_size("seq")
    rep = shards // head_count
    length = shards * row_count
    me = lax.axis_index("seq")
    head, part = me // rep, me % rep
    part_rows = length // rep

    def columns(weights):
        return lax.dynamic_slice_in_dim(weights, head * HEAD_DIM, HEAD_DIM, axis=2)

    mine = jnp.concatenate([columns(target_qkv), columns(student_qkv)], axis=0)
    weights = both_of_dp(mine, 1)
    relaid = both_of_dp(student_out, 1)

    grp = lax.axis_index("grp")
    half_rows = row_count // 2
    own_tokens = lax.dynamic_slice_in_dim(clips[0], grp * half_rows, half_rows, axis=0)
    own_tokens = own_tokens.astype(jnp.float32)
    normed = layer_norm(own_tokens)[0].astype(jnp.bfloat16)
    tables = position_tables(length, width)
    small = jnp.concatenate([context[0], predict_index[0]])[None, :]
    small = jnp.pad(small, ((0, 7), (0, -small.shape[1] % 128)))
    every, small, seed_normed = gather_rows(normed, shards, small, tables, mask_token)
    small = small[:, 0]
    flags = small[:, :row_count]
    lists = small[:, row_count : row_count + predict_index.shape[1]].reshape(-1)

    def own_part(rows):
        if rep == 1:
            return rows
        return lax.dynamic_slice_in_dim(rows, part * part_rows, part_rows, axis=0)

    def project(rows, some):
        return jnp.einsum(
            "nr,krc->knc", rows, some, preferred_element_type=jnp.float32
        ).astype(jnp.bfloat16)

    seed_queries = dot32(own_part(seed_normed), weights[3]).astype(jnp.bfloat16)
    if rep == 1:
        query_t, key_t, value_t = project(every, weights[:3])
    else:
        query_t = dot32(own_part(every), weights[0]).astype(jnp.bfloat16)
        key_t, value_t = project(every, weights[1:3])

    is_context = flags == 1
    order = jnp.cumsum(is_context.astype(jnp.int32), axis=1) - 1
    selector = (
        (order[:, None, :] == jnp.arange(CTX_DEV, dtype=jnp.int32)[None, :, None])
        & is_context[:, None, :]
    ).astype(jnp.bfloat16)
    chosen = jnp.einsum(
        "sck,skw->scw",
        selector,
        every.reshape(shards, row_count, width),
        preferred_element_type=jnp.float32,
    ).astype(jnp.bfloat16)
    chosen = chosen.reshape(shards * CTX_DEV, width)
    key_s, value_s = project(chosen, weights[4:])

    base = me * row_count + grp * half_rows
    first, second, twice_c, twice_s = tables
    blocks = half_rows // STRIDE
    first = lax.dynamic_slice_in_dim(first, base // STRIDE, blocks, axis=0)
    second = lax.dynamic_slice_in_dim(second, base // STRIDE, blocks, axis=0)
    own_seeds = first[:, None] * twice_c[None] + second[:, None] * twice_s[None]
    own_seeds = mask_token[None, :] + own_seeds.reshape(half_rows, width)
    places = base + jnp.arange(half_rows, dtype=jnp.int32)
    usable = jnp.sum(
        (lists[None, :] == places[:, None]).astype(jnp.float32), axis=1, keepdims=True
    )
    if rep == 1:
        blocked = (shards, row_count, HEAD_DIM)
        back_grad, student_mixed = middle(
            shards,
            [
                query_t.reshape(blocked), key_t, value_t,
                seed_queries.reshape(blocked), key_s, value_s,
                target_out, relaid, own_tokens, own_seeds, usable,
            ],
        )
        student_mixed = student_mixed.reshape(length, HEAD_DIM)
    else:
        target_mixed = attend(query_t, key_t, value_t)
        student_mixed = attend(seed_queries, key_s, value_s)
        both = jnp.concatenate([target_mixed, student_mixed], axis=1)
        if rep == 1:
            both = both.reshape(shards, row_count, 2 * HEAD_DIM)
            both = lax.all_to_all(both, "seq", split_axis=0, concat_axis=0, tiled=True)
        else:
            both = lax.all_gather(both, "seq", axis=0, tiled=True)
            both = both.reshape(head_count, length, 2 * HEAD_DIM)
            both = lax.dynamic_slice_in_dim(both, me * row_count, row_count, axis=1)
        own_target = both[:, :, :HEAD_DIM].transpose(1, 0, 2).reshape(row_count, half_width)
        own_student = both[:, :, HEAD_DIM:].transpose(1, 0, 2).reshape(row_count, half_width)
        sums = jnp.stack(
            [
                dot32(own_target, target_out).astype(jnp.bfloat16),
                dot32(own_student, relaid).astype(jnp.bfloat16),
            ]
        )
        low, high = sums[:, :half_rows], sums[:, half_rows:]
        keep, send = jnp.where(grp == 0, low, high), jnp.where(grp == 0, high, low)
        came = lax.ppermute(send, "grp", [(0, 1), (1, 0)])
        sums = keep.astype(jnp.float32) + came.astype(jnp.float32)

        features = layer_norm(own_tokens + sums[0])[0].astype(jnp.bfloat16)
        predicted, factor = layer_norm(own_seeds + sums[1])
        back_grad = gradient(predicted, factor, features, usable)
    back_all = gather_rows(back_grad.astype(jnp.bfloat16), shards)[0]
    head_grad = lax.dot_general(
        student_mixed,
        own_part(back_all),
        (((0,), (0,)), ((), ())),
        preferred_element_type=jnp.float32,
    ).astype(jnp.bfloat16)
    if lax.axis_size("dp") == 2:
        half = head_grad.shape[1] // 2
        first = lax.axis_index("dp") == 0
        low, high = head_grad[:, :half], head_grad[:, half:]
        keep, send = jnp.where(first, low, high), jnp.where(first, high, low)
        came = lax.ppermute(send, "dp", [(0, 1), (1, 0)])
        head_grad = (keep.astype(jnp.float32) + came.astype(jnp.float32)).astype(jnp.bfloat16)
    else:
        head_grad = lax.psum_scatter(head_grad, "dp", scatter_dimension=1, tiled=True)
    out_grad = lax.all_gather(head_grad, "seq", axis=0, tiled=True).astype(jnp.float32)
    if rep > 1:
        out_grad = out_grad.reshape(head_count, rep, HEAD_DIM, -1).sum(1)
        out_grad = out_grad.reshape(half_width, -1)
    target_blend = MOMENTUM * target_out.astype(jnp.float32) + (1.0 - MOMENTUM) * relaid.astype(
        jnp.float32
    )
    return (out_grad, target_blend)


def solution(mesh):
    in_specs = (
        P("dp", "seq", None),
        P("dp", "seq"),
        P("dp", "seq"),
        P(None, "dp", "grp"),
        P("grp", None),
        P(None, "dp", "grp"),
        P("grp", "dp"),
        P(),
    )
    out_specs = (P("grp", "dp"), P("grp", None))
    return jax.shard_map(body, mesh=mesh, in_specs=in_specs, out_specs=out_specs, check_vma=False)
```

```python
import functools
import math

import jax
import jax.numpy as jnp
from jax import lax
from jax.experimental import pallas as pl
from jax.experimental.pallas import tpu as pltpu
from jax.sharding import PartitionSpec as P

MESH = pl.DeviceIdType.MESH
CHUNKS = 2

HEAD_DIM = 88
CTX_DEV = 32
EPSILON = 1e-06
MOMENTUM = 0.99
STRIDE = 32


def layer_norm(values):
    center = values - jnp.mean(values, axis=-1, keepdims=True)
    factor = lax.rsqrt(jnp.mean(center * center, axis=-1, keepdims=True) + EPSILON)
    return (center * factor, factor)


def position_tables(length, width):
    half_width = width // 2
    spacing = jnp.exp(jnp.arange(half_width, dtype=jnp.float32) * (-math.log(10000.0) / half_width))
    high = (jnp.arange(length // STRIDE) * STRIDE).astype(jnp.float32)[:, None] * spacing[None, :]
    low = jnp.arange(STRIDE).astype(jnp.float32)[:, None] * spacing[None, :]
    sin_h, cos_h = jnp.sin(high), jnp.cos(high)
    sin_l, cos_l = jnp.sin(low), jnp.cos(low)
    return (
        jnp.concatenate([sin_h, cos_h], axis=1),
        jnp.concatenate([cos_h, -sin_h], axis=1),
        jnp.concatenate([cos_l, cos_l], axis=1),
        jnp.concatenate([sin_l, sin_l], axis=1),
    )


def norm_seed_block(index, tables, mask_ref, seed_out):
    first, second, twice_c, twice_s = tables
    rows = pl.ds(index, 1)
    seeds = mask_ref[...] + (first[rows, :] * twice_c[...] + second[rows, :] * twice_s[...])
    start = pl.multiple_of(index * STRIDE, STRIDE)
    seed_out[pl.ds(start, STRIDE), :] = layer_norm(seeds)[0].astype(jnp.bfloat16)


def gather_kernel(shards, with_seeds, *refs):
    if with_seeds:
        (x_ref, small_ref, *tables, mask_ref, out_ref, small_out, seed_out) = refs[:10]
        sems = refs[10:]
        s_send, s_recv, s_own = sems[7:]
    else:
        x_ref, out_ref = refs[:2]
        sems = refs[2:]
    own_sem, z_send, z_recv, m_send, m_recv, y_send, y_recv = sems[:7]
    me, grp = lax.axis_index("seq"), lax.axis_index("grp")
    z, core = me // 2, me % 2
    depth = shards // 2
    mate, across = z * 2 + (1 - core), 1 - grp
    pieces = range(CHUNKS)

    barrier = pltpu.get_barrier_semaphore()
    if with_seeds:
        for k in range(1, shards):
            peer = {"seq": lax.rem(me + k, shards)}
            pl.semaphore_signal(barrier, inc=1, device_id=peer, device_id_type=MESH)
        greeted = shards - 1
    else:
        for k in range(1, depth):
            peer = {"seq": lax.rem(z + k, depth) * 2 + core}
            pl.semaphore_signal(barrier, inc=1, device_id=peer, device_id_type=MESH)
        pl.semaphore_signal(barrier, inc=1, device_id={"seq": mate}, device_id_type=MESH)
        greeted = depth
    pl.semaphore_signal(barrier, inc=1, device_id={"grp": across}, device_id_type=MESH)
    pl.semaphore_wait(barrier, greeted + 1)

    def remote(src, slot, group, piece, send, recv, to):
        return pltpu.make_async_remote_copy(
            src_ref=src,
            dst_ref=out_ref.at[slot, group, piece],
            send_sem=send,
            recv_sem=recv,
            device_id=to,
            device_id_type=MESH,
        )

    def z_copy(way, dist, piece):
        sign = 1 - 2 * way
        slot = (z - sign * (dist - 1)) * 2 + core
        src = x_ref.at[piece] if dist == 1 else out_ref.at[slot, grp, piece]
        return remote(
            src, slot, grp, piece,
            z_send.at[way, dist - 1, piece], z_recv.at[way, dist - 1, piece],
            {"seq": (z + sign) * 2 + core},
        )

    def comes(way, dist):
        return z >= dist if way == 0 else z + dist < depth

    def leaves(way):
        return z + 1 < depth if way == 0 else z >= 1

    def goes(way, dist):
        return leaves(way) if dist == 1 else leaves(way) & comes(way, dist - 1)

    def mate_copy(src, source, side, piece):
        group = grp if side == 0 else across
        return remote(
            src, source * 2 + core, group, piece,
            m_send.at[side, source, piece], m_recv.at[side, source, piece], {"seq": mate},
        )

    def y_copy(src, source, piece):
        return remote(
            src, source * 2 + core, grp, piece,
            y_send.at[source, piece], y_recv.at[source, piece], {"grp": across},
        )

    def small_copy(k):
        return pltpu.make_async_remote_copy(
            src_ref=small_ref,
            dst_ref=small_out.at[me],
            send_sem=s_send.at[k - 1],
            recv_sem=s_recv.at[k - 1],
            device_id={"seq": lax.rem(me + k, shards)},
            device_id_type=MESH,
        )

    for way in range(2):

        @pl.when(goes(way, 1))
        def _():
            for piece in pieces:
                z_copy(way, 1, piece).start()

    for piece in pieces:
        y_copy(x_ref.at[piece], z, piece).start()
        mate_copy(x_ref.at[piece], z, 0, piece).start()
    own = pltpu.make_async_copy(x_ref, out_ref.at[me, grp], own_sem)
    own.start()
    if with_seeds:
        for k in range(1, shards):
            small_copy(k).start()
        small_own = pltpu.make_async_copy(small_ref, small_out.at[me], s_own)
        small_own.start()
        blocks = seed_out.shape[0] // STRIDE
        stages = depth + 1

    def work(stage):
        if with_seeds:
            lax.fori_loop(
                stage * blocks // stages,
                (stage + 1) * blocks // stages,
                lambda i, _: (norm_seed_block(i, tables, mask_ref, seed_out), 0)[1],
                0,
            )

    def from_z(way, dist):
        source = z - dist if way == 0 else z + dist

        @pl.when(comes(way, dist))
        def _():
            for piece in pieces:
                z_copy(way, dist, piece).wait_recv()
                if dist + 1 < depth:

                    @pl.when(leaves(way))
                    def _():
                        z_copy(way, dist + 1, piece).start()

                held = out_ref.at[source * 2 + core, grp, piece]
                y_copy(held, source, piece).start()
                mate_copy(held, source, 0, piece).start()

    def from_y(source):
        for piece in pieces:
            held = out_ref.at[source * 2 + core, across, piece]
            y_copy(held, source, piece).wait_recv()
            mate_copy(held, source, 1, piece).start()

    work(0)
    from_y(z)
    for dist in range(1, depth):
        work(dist)
        for way in range(2):
            from_z(way, dist)
        if dist > 1:
            for way in range(2):

                @pl.when(comes(way, dist - 1))
                def _():
                    from_y(z - (dist - 1) if way == 0 else z + (dist - 1))

    work(depth)
    for way in range(2):

        @pl.when(comes(way, depth - 1))
        def _():
            from_y(z - (depth - 1) if way == 0 else z + (depth - 1))

    for source in range(depth):
        for piece in pieces:
            for side in range(2):
                mate_copy(out_ref.at[source * 2 + core, grp, piece], source, side, piece).wait()
            y_copy(out_ref.at[source * 2 + core, grp, piece], source, piece).wait_send()
    for dist in range(1, depth):
        for way in range(2):

            @pl.when(goes(way, dist))
            def _():
                for piece in pieces:
                    z_copy(way, dist, piece).wait_send()

    own.wait()
    if with_seeds:
        for k in range(1, shards):
            small_copy(k).wait()
        small_own.wait()


def gather_rows(rows, shards, small=None, tables=None, mask=None):
    count, width = rows.shape
    depth = shards // 2
    dma = pltpu.SemaphoreType.DMA
    shaped = rows.reshape(CHUNKS, count // CHUNKS, width)
    out_shape = [jax.ShapeDtypeStruct((shards, 2) + shaped.shape, rows.dtype)]
    operands = [shaped]
    scratch = [
        dma,
        dma((2, depth - 1, CHUNKS)),
        dma((2, depth - 1, CHUNKS)),
        dma((2, depth, CHUNKS)),
        dma((2, depth, CHUNKS)),
        dma((depth, CHUNKS)),
        dma((depth, CHUNKS)),
    ]
    with_seeds = small is not None
    if with_seeds:
        operands += [small, *tables, mask[None, :]]
        out_shape += [
            jax.ShapeDtypeStruct((shards,) + small.shape, small.dtype),
            jax.ShapeDtypeStruct((tables[0].shape[0] * STRIDE, width), jnp.bfloat16),
        ]
        scratch += [dma((shards - 1,)), dma((shards - 1,)), dma]
    vmem = pl.BlockSpec(memory_space=pltpu.VMEM)
    results = pl.pallas_call(
        functools.partial(gather_kernel, shards, with_seeds),
        out_shape=out_shape,
        in_specs=[vmem] * len(operands),
        out_specs=[vmem] * len(out_shape),
        scratch_shapes=scratch,
        name="gather_seeds" if with_seeds else "gather_rows",
        compiler_params=pltpu.CompilerParams(
            collective_id=1 if with_seeds else 2,
            has_side_effects=True,
            vmem_limit_bytes=48 * 1024 * 1024,
        ),
    )(*operands)
    return (results[0].reshape(shards * 2 * count, width), *results[1:])


def middle_kernel(shards, *refs):
    (
        every, seeded, chosen, weights, out_t, out_s, tokens_ref, seeds_ref, usable_ref,
        back_ref, mix_s, k_t, v_t, k_s, v_s, mix_t, got_t, got_s, part_t, part_s, came_t, came_s,
        send_t, recv_t, send_s, recv_s, y_send, y_recv,
    ) = refs
    me, grp = lax.axis_index("seq"), lax.axis_index("grp")
    across = 1 - grp

    barrier = pltpu.get_barrier_semaphore()
    for k in range(1, shards):
        peer = {"seq": lax.rem(me + k, shards)}
        pl.semaphore_signal(barrier, inc=1, device_id=peer, device_id_type=MESH)
    pl.semaphore_signal(barrier, inc=1, device_id={"grp": across}, device_id_type=MESH)
    pl.semaphore_wait(barrier, shards)

    def turn(k):
        return lax.rem(me + 1 + k, shards)

    def copy(k, mix, got, send, recv):
        return pltpu.make_async_remote_copy(
            src_ref=mix.at[turn(k)],
            dst_ref=got.at[me],
            send_sem=send.at[k],
            recv_sem=recv.at[k],
            device_id={"seq": turn(k)},
            device_id_type=MESH,
        )

    def narrow(rows, index):
        return dot32(rows, weights[index]).astype(jnp.bfloat16)

    def heads(source, index, keys, values, mix, got, send, recv):
        def step(k, carry):
            dest = turn(k)
            queries = narrow(source[dest], index)
            mix[dest] = attend(queries, keys[...], values[...])

            @pl.when(k > 0)
            def _():
                copy(k - 1, mix, got, send, recv).start()

            return carry

        lax.fori_loop(0, shards, step, 0)
        got[me] = mix[me]

    def y_copy(index, part, came):
        return pltpu.make_async_remote_copy(
            src_ref=part.at[across],
            dst_ref=came,
            send_sem=y_send.at[index],
            recv_sem=y_recv.at[index],
            device_id={"grp": across},
            device_id_type=MESH,
        )

    def project(got, weights, part):
        rows = jnp.concatenate([got[k] for k in range(shards)], axis=1)
        whole = dot32(rows, weights[...]).astype(jnp.bfloat16)
        half = whole.shape[0] // 2
        part[0] = whole[:half]
        part[1] = whole[half:]

    def total(part, came):
        return part[grp].astype(jnp.float32) + came[...].astype(jnp.float32)

    def pair(k, carry):
        rows = pl.ds(pl.multiple_of(k * every.shape[1], every.shape[1]), every.shape[1])
        k_t[rows, :] = narrow(every[k], 1)
        v_t[rows, :] = narrow(every[k], 2)
        return carry

    lax.fori_loop(0, shards, pair, 0)
    heads(every, 0, k_t, v_t, mix_t, got_t, send_t, recv_t)
    k_s[...] = narrow(chosen[...], 4)
    v_s[...] = narrow(chosen[...], 5)
    heads(seeded, 3, k_s, v_s, mix_s, got_s, send_s, recv_s)
    for k in range(shards - 1):
        copy(k, mix_t, got_t, send_t, recv_t).wait_recv()
    project(got_t, out_t, part_t)
    copy(0, mix_s, got_s, send_s, recv_s).wait_recv()
    y_copy(0, part_t, came_t).start()
    for k in range(1, shards - 1):
        copy(k, mix_s, got_s, send_s, recv_s).wait_recv()
    project(got_s, out_s, part_s)
    y_copy(0, part_t, came_t).wait_recv()
    y_copy(1, part_s, came_s).start()
    tokens = tokens_ref[...].astype(jnp.float32)
    features = layer_norm(tokens + total(part_t, came_t))[0].astype(jnp.bfloat16)
    y_copy(1, part_s, came_s).wait_recv()
    predicted, factor = layer_norm(seeds_ref[...] + total(part_s, came_s))
    back_ref[...] = gradient(predicted, factor, features, usable_ref[...]).astype(jnp.bfloat16)
    for k in range(shards - 1):
        copy(k, mix_t, got_t, send_t, recv_t).wait_send()
        copy(k, mix_s, got_s, send_s, recv_s).wait_send()
    y_copy(0, part_t, came_t).wait_send()
    y_copy(1, part_s, came_s).wait_send()


def middle(shards, operands):
    blocked = operands[0].shape[:2] + (HEAD_DIM,)
    flat = (blocked[0] * blocked[1], HEAD_DIM)
    some = (operands[2].shape[0], HEAD_DIM)
    rows, width = operands[6].shape
    bf16, dma = jnp.bfloat16, pltpu.SemaphoreType.DMA
    vmem = pl.BlockSpec(memory_space=pltpu.VMEM)
    return pl.pallas_call(
        functools.partial(middle_kernel, shards),
        out_shape=[
            jax.ShapeDtypeStruct((rows, width), bf16),
            jax.ShapeDtypeStruct(blocked, bf16),
        ],
        in_specs=[vmem] * len(operands),
        out_specs=[vmem] * 2,
        scratch_shapes=[pltpu.VMEM(flat, bf16)] * 2
        + [pltpu.VMEM(some, bf16)] * 2
        + [pltpu.VMEM(blocked, bf16)] * 3
        + [pltpu.VMEM((2, rows, width), bf16)] * 2
        + [pltpu.VMEM((rows, width), bf16)] * 2
        + [dma((shards - 1,))] * 4
        + [dma((2,))] * 2,
        name="middle",
        compiler_params=pltpu.CompilerParams(
            collective_id=3, has_side_effects=True, vmem_limit_bytes=48 * 1024 * 1024
        ),
    )(*operands)


def gradient(predicted, factor, features, usable):
    slope = jnp.clip(predicted - features.astype(jnp.float32), -1.0, 1.0) * usable
    return (
        slope
        - jnp.mean(slope, axis=1, keepdims=True)
        - predicted * jnp.mean(slope * predicted, axis=1, keepdims=True)
    ) * factor


def attend(queries, keys, values):
    scores = lax.dot_general(
        queries, keys, (((1,), (1,)), ((), ())), preferred_element_type=jnp.float32
    ) * (HEAD_DIM ** (-0.5))
    shifted = jnp.exp(scores - jnp.max(scores, axis=1, keepdims=True))
    totals = jnp.sum(shifted, axis=1, keepdims=True)
    summed = jnp.dot(shifted.astype(jnp.bfloat16), values, preferred_element_type=jnp.float32)
    return (summed / totals).astype(jnp.bfloat16)


def dot32(left, right):
    return jnp.dot(left, right, preferred_element_type=jnp.float32)


def both_of_dp(block, axis):
    if lax.axis_size("dp") != 2:
        return lax.all_gather(block, "dp", axis=axis, tiled=True)
    other = lax.ppermute(block, "dp", [(0, 1), (1, 0)])
    first = lax.axis_index("dp") == 0
    return jnp.concatenate(
        [jnp.where(first, block, other), jnp.where(first, other, block)], axis=axis
    )


def body(
    clips, context, predict_index, target_qkv, target_out, student_qkv, student_out, mask_token
):
    row_count, width = clips.shape[1:]
    half_width = target_qkv.shape[2]
    head_count = half_width // HEAD_DIM
    shards = lax.axis_size("seq")
    rep = shards // head_count
    length = shards * row_count
    me = lax.axis_index("seq")
    head, part = me // rep, me % rep
    part_rows = length // rep

    def columns(weights):
        return lax.dynamic_slice_in_dim(weights, head * HEAD_DIM, HEAD_DIM, axis=2)

    mine = jnp.concatenate([columns(target_qkv), columns(student_qkv)], axis=0)
    weights = both_of_dp(mine, 1)
    relaid = both_of_dp(student_out, 1)

    grp = lax.axis_index("grp")
    half_rows = row_count // 2
    own_tokens = lax.dynamic_slice_in_dim(clips[0], grp * half_rows, half_rows, axis=0)
    own_tokens = own_tokens.astype(jnp.float32)
    normed = layer_norm(own_tokens)[0].astype(jnp.bfloat16)
    tables = position_tables(length, width)
    small = jnp.concatenate([context[0], predict_index[0]])[None, :]
    small = jnp.pad(small, ((0, 7), (0, -small.shape[1] % 128)))
    every, small, seed_normed = gather_rows(normed, shards, small, tables, mask_token)
    small = small[:, 0]
    flags = small[:, :row_count]
    lists = small[:, row_count : row_count + predict_index.shape[1]].reshape(-1)

    def own_part(rows):
        if rep == 1:
            return rows
        return lax.dynamic_slice_in_dim(rows, part * part_rows, part_rows, axis=0)

    def project(rows, some):
        return jnp.einsum(
            "nr,krc->knc", rows, some, preferred_element_type=jnp.float32
        ).astype(jnp.bfloat16)

    is_context = flags == 1
    order = jnp.cumsum(is_context.astype(jnp.int32), axis=1) - 1
    selector = (
        (order[:, None, :] == jnp.arange(CTX_DEV, dtype=jnp.int32)[None, :, None])
        & is_context[:, None, :]
    ).astype(jnp.bfloat16)
    chosen = jnp.einsum(
        "sck,skw->scw",
        selector,
        every.reshape(shards, row_count, width),
        preferred_element_type=jnp.float32,
    ).astype(jnp.bfloat16)
    chosen = chosen.reshape(shards * CTX_DEV, width)

    base = me * row_count + grp * half_rows
    first, second, twice_c, twice_s = tables
    blocks = half_rows // STRIDE
    first = lax.dynamic_slice_in_dim(first, base // STRIDE, blocks, axis=0)
    second = lax.dynamic_slice_in_dim(second, base // STRIDE, blocks, axis=0)
    own_seeds = first[:, None] * twice_c[None] + second[:, None] * twice_s[None]
    own_seeds = mask_token[None, :] + own_seeds.reshape(half_rows, width)
    places = base + jnp.arange(half_rows, dtype=jnp.int32)
    usable = jnp.sum(
        (lists[None, :] == places[:, None]).astype(jnp.float32), axis=1, keepdims=True
    )
    if rep == 1:
        blocked = (shards, row_count, width)
        back_grad, student_mixed = middle(
            shards,
            [
                every.reshape(blocked), seed_normed.reshape(blocked), chosen, weights,
                target_out, relaid, own_tokens, own_seeds, usable,
            ],
        )
        student_mixed = student_mixed.reshape(length, HEAD_DIM)
    else:
        query_t = dot32(own_part(every), weights[0]).astype(jnp.bfloat16)
        key_t, value_t = project(every, weights[1:3])
        seed_queries = dot32(own_part(seed_normed), weights[3]).astype(jnp.bfloat16)
        key_s, value_s = project(chosen, weights[4:])
        target_mixed = attend(query_t, key_t, value_t)
        student_mixed = attend(seed_queries, key_s, value_s)
        both = jnp.concatenate([target_mixed, student_mixed], axis=1)
        if rep == 1:
            both = both.reshape(shards, row_count, 2 * HEAD_DIM)
            both = lax.all_to_all(both, "seq", split_axis=0, concat_axis=0, tiled=True)
        else:
            both = lax.all_gather(both, "seq", axis=0, tiled=True)
            both = both.reshape(head_count, length, 2 * HEAD_DIM)
            both = lax.dynamic_slice_in_dim(both, me * row_count, row_count, axis=1)
        own_target = both[:, :, :HEAD_DIM].transpose(1, 0, 2).reshape(row_count, half_width)
        own_student = both[:, :, HEAD_DIM:].transpose(1, 0, 2).reshape(row_count, half_width)
        sums = jnp.stack(
            [
                dot32(own_target, target_out).astype(jnp.bfloat16),
                dot32(own_student, relaid).astype(jnp.bfloat16),
            ]
        )
        low, high = sums[:, :half_rows], sums[:, half_rows:]
        keep, send = jnp.where(grp == 0, low, high), jnp.where(grp == 0, high, low)
        came = lax.ppermute(send, "grp", [(0, 1), (1, 0)])
        sums = keep.astype(jnp.float32) + came.astype(jnp.float32)

        features = layer_norm(own_tokens + sums[0])[0].astype(jnp.bfloat16)
        predicted, factor = layer_norm(own_seeds + sums[1])
        back_grad = gradient(predicted, factor, features, usable)
    back_all = gather_rows(back_grad.astype(jnp.bfloat16), shards)[0]
    head_grad = lax.dot_general(
        student_mixed,
        own_part(back_all),
        (((0,), (0,)), ((), ())),
        preferred_element_type=jnp.float32,
    ).astype(jnp.bfloat16)
    if lax.axis_size("dp") == 2:
        half = head_grad.shape[1] // 2
        first = lax.axis_index("dp") == 0
        low, high = head_grad[:, :half], head_grad[:, half:]
        keep, send = jnp.where(first, low, high), jnp.where(first, high, low)
        came = lax.ppermute(send, "dp", [(0, 1), (1, 0)])
        head_grad = (keep.astype(jnp.float32) + came.astype(jnp.float32)).astype(jnp.bfloat16)
    else:
        head_grad = lax.psum_scatter(head_grad, "dp", scatter_dimension=1, tiled=True)
    out_grad = lax.all_gather(head_grad, "seq", axis=0, tiled=True).astype(jnp.float32)
    if rep > 1:
        out_grad = out_grad.reshape(head_count, rep, HEAD_DIM, -1).sum(1)
        out_grad = out_grad.reshape(half_width, -1)
    target_blend = MOMENTUM * target_out.astype(jnp.float32) + (1.0 - MOMENTUM) * relaid.astype(
        jnp.float32
    )
    return (out_grad, target_blend)


def solution(mesh):
    in_specs = (
        P("dp", "seq", None),
        P("dp", "seq"),
        P("dp", "seq"),
        P(None, "dp", "grp"),
        P("grp", None),
        P(None, "dp", "grp"),
        P("grp", "dp"),
        P(),
    )
    out_specs = (P("grp", "dp"), P("grp", None))
    return jax.shard_map(body, mesh=mesh, in_specs=in_specs, out_specs=out_specs, check_vma=False)
```

```python
import functools
import math

import jax
import jax.numpy as jnp
from jax import lax
from jax.experimental import pallas as pl
from jax.experimental.pallas import tpu as pltpu
from jax.sharding import PartitionSpec as P

MESH = pl.DeviceIdType.MESH
CHUNKS = 2

HEAD_DIM = 88
CTX_DEV = 32
EPSILON = 1e-06
MOMENTUM = 0.99
STRIDE = 32


def layer_norm(values):
    center = values - jnp.mean(values, axis=-1, keepdims=True)
    factor = lax.rsqrt(jnp.mean(center * center, axis=-1, keepdims=True) + EPSILON)
    return (center * factor, factor)


def position_tables(length, width):
    half_width = width // 2
    spacing = jnp.exp(jnp.arange(half_width, dtype=jnp.float32) * (-math.log(10000.0) / half_width))
    high = (jnp.arange(length // STRIDE) * STRIDE).astype(jnp.float32)[:, None] * spacing[None, :]
    low = jnp.arange(STRIDE).astype(jnp.float32)[:, None] * spacing[None, :]
    sin_h, cos_h = jnp.sin(high), jnp.cos(high)
    sin_l, cos_l = jnp.sin(low), jnp.cos(low)
    return (
        jnp.concatenate([sin_h, cos_h], axis=1),
        jnp.concatenate([cos_h, -sin_h], axis=1),
        jnp.concatenate([cos_l, cos_l], axis=1),
        jnp.concatenate([sin_l, sin_l], axis=1),
    )


def norm_seed_block(index, tables, mask_ref, seed_out):
    first, second, twice_c, twice_s = tables
    rows = pl.ds(index, 1)
    seeds = mask_ref[...] + (first[rows, :] * twice_c[...] + second[rows, :] * twice_s[...])
    start = pl.multiple_of(index * STRIDE, STRIDE)
    seed_out[pl.ds(start, STRIDE), :] = layer_norm(seeds)[0].astype(jnp.bfloat16)


def gather_kernel(shards, with_seeds, *refs):
    if with_seeds:
        (x_ref, small_ref, *tables, mask_ref, out_ref, small_out, seed_out) = refs[:10]
        sems = refs[10:]
        s_send, s_recv, s_own = sems[7:]
    else:
        x_ref, out_ref = refs[:2]
        sems = refs[2:]
    own_sem, z_send, z_recv, m_send, m_recv, y_send, y_recv = sems[:7]
    me, grp = lax.axis_index("seq"), lax.axis_index("grp")
    z, core = me // 2, me % 2
    depth = shards // 2
    mate, across = z * 2 + (1 - core), 1 - grp
    pieces = range(CHUNKS)

    barrier = pltpu.get_barrier_semaphore()
    if with_seeds:
        for k in range(1, shards):
            peer = {"seq": lax.rem(me + k, shards)}
            pl.semaphore_signal(barrier, inc=1, device_id=peer, device_id_type=MESH)
        greeted = shards - 1
    else:
        for k in range(1, depth):
            peer = {"seq": lax.rem(z + k, depth) * 2 + core}
            pl.semaphore_signal(barrier, inc=1, device_id=peer, device_id_type=MESH)
        pl.semaphore_signal(barrier, inc=1, device_id={"seq": mate}, device_id_type=MESH)
        greeted = depth
    pl.semaphore_signal(barrier, inc=1, device_id={"grp": across}, device_id_type=MESH)
    pl.semaphore_wait(barrier, greeted + 1)

    def remote(src, slot, group, piece, send, recv, to):
        return pltpu.make_async_remote_copy(
            src_ref=src,
            dst_ref=out_ref.at[slot, group, piece],
            send_sem=send,
            recv_sem=recv,
            device_id=to,
            device_id_type=MESH,
        )

    def z_copy(way, dist, piece):
        sign = 1 - 2 * way
        slot = (z - sign * (dist - 1)) * 2 + core
        src = x_ref.at[piece] if dist == 1 else out_ref.at[slot, grp, piece]
        return remote(
            src, slot, grp, piece,
            z_send.at[way, dist - 1, piece], z_recv.at[way, dist - 1, piece],
            {"seq": (z + sign) * 2 + core},
        )

    def comes(way, dist):
        return z >= dist if way == 0 else z + dist < depth

    def leaves(way):
        return z + 1 < depth if way == 0 else z >= 1

    def goes(way, dist):
        return leaves(way) if dist == 1 else leaves(way) & comes(way, dist - 1)

    def mate_copy(src, source, side, piece):
        group = grp if side == 0 else across
        return remote(
            src, source * 2 + core, group, piece,
            m_send.at[side, source, piece], m_recv.at[side, source, piece], {"seq": mate},
        )

    def y_copy(src, source, piece):
        return remote(
            src, source * 2 + core, grp, piece,
            y_send.at[source, piece], y_recv.at[source, piece], {"grp": across},
        )

    def small_copy(k):
        return pltpu.make_async_remote_copy(
            src_ref=small_ref,
            dst_ref=small_out.at[me],
            send_sem=s_send.at[k - 1],
            recv_sem=s_recv.at[k - 1],
            device_id={"seq": lax.rem(me + k, shards)},
            device_id_type=MESH,
        )

    for way in range(2):

        @pl.when(goes(way, 1))
        def _():
            for piece in pieces:
                z_copy(way, 1, piece).start()

    for piece in pieces:
        y_copy(x_ref.at[piece], z, piece).start()
        mate_copy(x_ref.at[piece], z, 0, piece).start()
    own = pltpu.make_async_copy(x_ref, out_ref.at[me, grp], own_sem)
    own.start()
    if with_seeds:
        for k in range(1, shards):
            small_copy(k).start()
        small_own = pltpu.make_async_copy(small_ref, small_out.at[me], s_own)
        small_own.start()
        blocks = seed_out.shape[0] // STRIDE
        stages = depth + 1

    def work(stage):
        if with_seeds:
            lax.fori_loop(
                stage * blocks // stages,
                (stage + 1) * blocks // stages,
                lambda i, _: (norm_seed_block(i, tables, mask_ref, seed_out), 0)[1],
                0,
            )

    def from_z(way, dist):
        source = z - dist if way == 0 else z + dist

        @pl.when(comes(way, dist))
        def _():
            for piece in pieces:
                z_copy(way, dist, piece).wait_recv()
                if dist + 1 < depth:

                    @pl.when(leaves(way))
                    def _():
                        z_copy(way, dist + 1, piece).start()

                held = out_ref.at[source * 2 + core, grp, piece]
                y_copy(held, source, piece).start()
                mate_copy(held, source, 0, piece).start()

    def from_y(source):
        for piece in pieces:
            held = out_ref.at[source * 2 + core, across, piece]
            y_copy(held, source, piece).wait_recv()
            mate_copy(held, source, 1, piece).start()

    work(0)
    from_y(z)
    for dist in range(1, depth):
        work(dist)
        for way in range(2):
            from_z(way, dist)
        if dist > 1:
            for way in range(2):

                @pl.when(comes(way, dist - 1))
                def _():
                    from_y(z - (dist - 1) if way == 0 else z + (dist - 1))

    work(depth)
    for way in range(2):

        @pl.when(comes(way, depth - 1))
        def _():
            from_y(z - (depth - 1) if way == 0 else z + (depth - 1))

    for source in range(depth):
        for piece in pieces:
            for side in range(2):
                mate_copy(out_ref.at[source * 2 + core, grp, piece], source, side, piece).wait()
            y_copy(out_ref.at[source * 2 + core, grp, piece], source, piece).wait_send()
    for dist in range(1, depth):
        for way in range(2):

            @pl.when(goes(way, dist))
            def _():
                for piece in pieces:
                    z_copy(way, dist, piece).wait_send()

    own.wait()
    if with_seeds:
        for k in range(1, shards):
            small_copy(k).wait()
        small_own.wait()


def gather_rows(rows, shards, small=None, tables=None, mask=None):
    count, width = rows.shape
    depth = shards // 2
    dma = pltpu.SemaphoreType.DMA
    shaped = rows.reshape(CHUNKS, count // CHUNKS, width)
    out_shape = [jax.ShapeDtypeStruct((shards, 2) + shaped.shape, rows.dtype)]
    operands = [shaped]
    scratch = [
        dma,
        dma((2, depth - 1, CHUNKS)),
        dma((2, depth - 1, CHUNKS)),
        dma((2, depth, CHUNKS)),
        dma((2, depth, CHUNKS)),
        dma((depth, CHUNKS)),
        dma((depth, CHUNKS)),
    ]
    with_seeds = small is not None
    if with_seeds:
        operands += [small, *tables, mask[None, :]]
        out_shape += [
            jax.ShapeDtypeStruct((shards,) + small.shape, small.dtype),
            jax.ShapeDtypeStruct((tables[0].shape[0] * STRIDE, width), jnp.bfloat16),
        ]
        scratch += [dma((shards - 1,)), dma((shards - 1,)), dma]
    vmem = pl.BlockSpec(memory_space=pltpu.VMEM)
    results = pl.pallas_call(
        functools.partial(gather_kernel, shards, with_seeds),
        out_shape=out_shape,
        in_specs=[vmem] * len(operands),
        out_specs=[vmem] * len(out_shape),
        scratch_shapes=scratch,
        name="gather_seeds" if with_seeds else "gather_rows",
        compiler_params=pltpu.CompilerParams(
            collective_id=1 if with_seeds else 2,
            has_side_effects=True,
            vmem_limit_bytes=48 * 1024 * 1024,
        ),
    )(*operands)
    return (results[0].reshape(shards * 2 * count, width), *results[1:])


def middle_kernel(shards, *refs):
    (
        every, seeded, chosen, weights, out_t, own_s, other_s, tokens_ref, seeds_ref, usable_ref,
        back_ref, mix_s, k_t, v_t, k_s, v_s, mix_t, got_t, got_s, part_t, part_s, came_t, came_s,
        send_t, recv_t, send_s, recv_s, y_send, y_recv,
    ) = refs
    me, grp = lax.axis_index("seq"), lax.axis_index("grp")
    across = 1 - grp

    barrier = pltpu.get_barrier_semaphore()
    for k in range(1, shards):
        peer = {"seq": lax.rem(me + k, shards)}
        pl.semaphore_signal(barrier, inc=1, device_id=peer, device_id_type=MESH)
    pl.semaphore_signal(barrier, inc=1, device_id={"grp": across}, device_id_type=MESH)
    pl.semaphore_wait(barrier, shards)

    def turn(k):
        return lax.rem(me + 1 + k, shards)

    def copy(k, mix, got, send, recv):
        return pltpu.make_async_remote_copy(
            src_ref=mix.at[turn(k)],
            dst_ref=got.at[me],
            send_sem=send.at[k],
            recv_sem=recv.at[k],
            device_id={"seq": turn(k)},
            device_id_type=MESH,
        )

    def narrow(rows, index):
        return dot32(rows, weights[index]).astype(jnp.bfloat16)

    def heads(source, index, keys, values, mix, got, send, recv):
        def step(k, carry):
            dest = turn(k)
            queries = narrow(source[dest], index)
            mix[dest] = attend(queries, keys[...], values[...])

            @pl.when(k > 0)
            def _():
                copy(k - 1, mix, got, send, recv).start()

            return carry

        lax.fori_loop(0, shards, step, 0)
        got[me] = mix[me]

    def y_copy(index, part, came):
        return pltpu.make_async_remote_copy(
            src_ref=part.at[across],
            dst_ref=came,
            send_sem=y_send.at[index],
            recv_sem=y_recv.at[index],
            device_id={"grp": across},
            device_id_type=MESH,
        )

    def joined(got):
        return jnp.concatenate([got[k] for k in range(shards)], axis=1)

    def place(columns, part):
        whole = jnp.concatenate(columns, axis=1).astype(jnp.bfloat16)
        half = whole.shape[0] // 2
        part[0] = whole[:half]
        part[1] = whole[half:]

    def total(part, came):
        return part[grp].astype(jnp.float32) + came[...].astype(jnp.float32)

    def pair(k, carry):
        rows = pl.ds(pl.multiple_of(k * every.shape[1], every.shape[1]), every.shape[1])
        k_t[rows, :] = narrow(every[k], 1)
        v_t[rows, :] = narrow(every[k], 2)
        return carry

    lax.fori_loop(0, shards, pair, 0)
    heads(every, 0, k_t, v_t, mix_t, got_t, send_t, recv_t)
    k_s[...] = narrow(chosen[...], 4)
    v_s[...] = narrow(chosen[...], 5)
    heads(seeded, 3, k_s, v_s, mix_s, got_s, send_s, recv_s)
    for k in range(shards - 1):
        copy(k, mix_t, got_t, send_t, recv_t).wait_recv()
    place([dot32(joined(got_t), out_t[...])], part_t)
    copy(0, mix_s, got_s, send_s, recv_s).wait_recv()
    y_copy(0, part_t, came_t).start()
    for k in range(1, shards - 1):
        copy(k, mix_s, got_s, send_s, recv_s).wait_recv()
    rows = joined(got_s)
    own_columns, other_columns = dot32(rows, own_s[...]), dot32(rows, other_s[...])
    first = lax.axis_index("dp") == 0

    @pl.when(first)
    def _():
        place([own_columns, other_columns], part_s)

    @pl.when(jnp.logical_not(first))
    def _():
        place([other_columns, own_columns], part_s)

    y_copy(0, part_t, came_t).wait_recv()
    y_copy(1, part_s, came_s).start()
    tokens = tokens_ref[...].astype(jnp.float32)
    features = layer_norm(tokens + total(part_t, came_t))[0].astype(jnp.bfloat16)
    y_copy(1, part_s, came_s).wait_recv()
    predicted, factor = layer_norm(seeds_ref[...] + total(part_s, came_s))
    back_ref[...] = gradient(predicted, factor, features, usable_ref[...]).astype(jnp.bfloat16)
    for k in range(shards - 1):
        copy(k, mix_t, got_t, send_t, recv_t).wait_send()
        copy(k, mix_s, got_s, send_s, recv_s).wait_send()
    y_copy(0, part_t, came_t).wait_send()
    y_copy(1, part_s, came_s).wait_send()


def middle(shards, operands):
    blocked = operands[0].shape[:2] + (HEAD_DIM,)
    flat = (blocked[0] * blocked[1], HEAD_DIM)
    some = (operands[2].shape[0], HEAD_DIM)
    rows, width = operands[7].shape
    bf16, dma = jnp.bfloat16, pltpu.SemaphoreType.DMA
    vmem = pl.BlockSpec(memory_space=pltpu.VMEM)
    return pl.pallas_call(
        functools.partial(middle_kernel, shards),
        out_shape=[
            jax.ShapeDtypeStruct((rows, width), bf16),
            jax.ShapeDtypeStruct(blocked, bf16),
        ],
        in_specs=[vmem] * len(operands),
        out_specs=[vmem] * 2,
        scratch_shapes=[pltpu.VMEM(flat, bf16)] * 2
        + [pltpu.VMEM(some, bf16)] * 2
        + [pltpu.VMEM(blocked, bf16)] * 3
        + [pltpu.VMEM((2, rows, width), bf16)] * 2
        + [pltpu.VMEM((rows, width), bf16)] * 2
        + [dma((shards - 1,))] * 4
        + [dma((2,))] * 2,
        name="middle",
        compiler_params=pltpu.CompilerParams(
            collective_id=3, has_side_effects=True, vmem_limit_bytes=48 * 1024 * 1024
        ),
    )(*operands)


def gradient(predicted, factor, features, usable):
    slope = jnp.clip(predicted - features.astype(jnp.float32), -1.0, 1.0) * usable
    return (
        slope
        - jnp.mean(slope, axis=1, keepdims=True)
        - predicted * jnp.mean(slope * predicted, axis=1, keepdims=True)
    ) * factor


def attend(queries, keys, values):
    scores = lax.dot_general(
        queries, keys, (((1,), (1,)), ((), ())), preferred_element_type=jnp.float32
    ) * (HEAD_DIM ** (-0.5))
    shifted = jnp.exp(scores - jnp.max(scores, axis=1, keepdims=True))
    totals = jnp.sum(shifted, axis=1, keepdims=True)
    summed = jnp.dot(shifted.astype(jnp.bfloat16), values, preferred_element_type=jnp.float32)
    return (summed / totals).astype(jnp.bfloat16)


def dot32(left, right):
    return jnp.dot(left, right, preferred_element_type=jnp.float32)


def swap(block):
    return lax.ppermute(block, "dp", [(0, 1), (1, 0)])


def both_of_dp(block, axis, other=None):
    if lax.axis_size("dp") != 2:
        return lax.all_gather(block, "dp", axis=axis, tiled=True)
    if other is None:
        other = swap(block)
    first = lax.axis_index("dp") == 0
    return jnp.concatenate(
        [jnp.where(first, block, other), jnp.where(first, other, block)], axis=axis
    )


def body(
    clips, context, predict_index, target_qkv, target_out, student_qkv, student_out, mask_token
):
    row_count, width = clips.shape[1:]
    half_width = target_qkv.shape[2]
    head_count = half_width // HEAD_DIM
    shards = lax.axis_size("seq")
    rep = shards // head_count
    length = shards * row_count
    me = lax.axis_index("seq")
    head, part = me // rep, me % rep
    part_rows = length // rep

    def columns(weights):
        return lax.dynamic_slice_in_dim(weights, head * HEAD_DIM, HEAD_DIM, axis=2)

    mine = jnp.concatenate([columns(target_qkv), columns(student_qkv)], axis=0)
    weights = both_of_dp(mine, 1)
    fused = rep == 1 and lax.axis_size("dp") == 2
    if fused:
        other_out = swap(student_out)
    else:
        relaid = both_of_dp(student_out, 1)

    grp = lax.axis_index("grp")
    half_rows = row_count // 2
    own_tokens = lax.dynamic_slice_in_dim(clips[0], grp * half_rows, half_rows, axis=0)
    own_tokens = own_tokens.astype(jnp.float32)
    normed = layer_norm(own_tokens)[0].astype(jnp.bfloat16)
    tables = position_tables(length, width)
    small = jnp.concatenate([context[0], predict_index[0]])[None, :]
    small = jnp.pad(small, ((0, 7), (0, -small.shape[1] % 128)))
    every, small, seed_normed = gather_rows(normed, shards, small, tables, mask_token)
    small = small[:, 0]
    flags = small[:, :row_count]
    lists = small[:, row_count : row_count + predict_index.shape[1]].reshape(-1)

    def own_part(rows):
        if rep == 1:
            return rows
        return lax.dynamic_slice_in_dim(rows, part * part_rows, part_rows, axis=0)

    def project(rows, some):
        return jnp.einsum(
            "nr,krc->knc", rows, some, preferred_element_type=jnp.float32
        ).astype(jnp.bfloat16)

    is_context = flags == 1
    order = jnp.cumsum(is_context.astype(jnp.int32), axis=1) - 1
    selector = (
        (order[:, None, :] == jnp.arange(CTX_DEV, dtype=jnp.int32)[None, :, None])
        & is_context[:, None, :]
    ).astype(jnp.bfloat16)
    chosen = jnp.einsum(
        "sck,skw->scw",
        selector,
        every.reshape(shards, row_count, width),
        preferred_element_type=jnp.float32,
    ).astype(jnp.bfloat16)
    chosen = chosen.reshape(shards * CTX_DEV, width)

    base = me * row_count + grp * half_rows
    first, second, twice_c, twice_s = tables
    blocks = half_rows // STRIDE
    first = lax.dynamic_slice_in_dim(first, base // STRIDE, blocks, axis=0)
    second = lax.dynamic_slice_in_dim(second, base // STRIDE, blocks, axis=0)
    own_seeds = first[:, None] * twice_c[None] + second[:, None] * twice_s[None]
    own_seeds = mask_token[None, :] + own_seeds.reshape(half_rows, width)
    places = base + jnp.arange(half_rows, dtype=jnp.int32)
    usable = jnp.sum(
        (lists[None, :] == places[:, None]).astype(jnp.float32), axis=1, keepdims=True
    )
    if fused:
        blocked = (shards, row_count, width)
        back_grad, student_mixed = middle(
            shards,
            [
                every.reshape(blocked), seed_normed.reshape(blocked), chosen, weights,
                target_out, student_out, other_out, own_tokens, own_seeds, usable,
            ],
        )
        student_mixed = student_mixed.reshape(length, HEAD_DIM)
    else:
        query_t = dot32(own_part(every), weights[0]).astype(jnp.bfloat16)
        key_t, value_t = project(every, weights[1:3])
        seed_queries = dot32(own_part(seed_normed), weights[3]).astype(jnp.bfloat16)
        key_s, value_s = project(chosen, weights[4:])
        target_mixed = attend(query_t, key_t, value_t)
        student_mixed = attend(seed_queries, key_s, value_s)
        both = jnp.concatenate([target_mixed, student_mixed], axis=1)
        if rep == 1:
            both = both.reshape(shards, row_count, 2 * HEAD_DIM)
            both = lax.all_to_all(both, "seq", split_axis=0, concat_axis=0, tiled=True)
        else:
            both = lax.all_gather(both, "seq", axis=0, tiled=True)
            both = both.reshape(head_count, length, 2 * HEAD_DIM)
            both = lax.dynamic_slice_in_dim(both, me * row_count, row_count, axis=1)
        own_target = both[:, :, :HEAD_DIM].transpose(1, 0, 2).reshape(row_count, half_width)
        own_student = both[:, :, HEAD_DIM:].transpose(1, 0, 2).reshape(row_count, half_width)
        sums = jnp.stack(
            [
                dot32(own_target, target_out).astype(jnp.bfloat16),
                dot32(own_student, relaid).astype(jnp.bfloat16),
            ]
        )
        low, high = sums[:, :half_rows], sums[:, half_rows:]
        keep, send = jnp.where(grp == 0, low, high), jnp.where(grp == 0, high, low)
        came = lax.ppermute(send, "grp", [(0, 1), (1, 0)])
        sums = keep.astype(jnp.float32) + came.astype(jnp.float32)

        features = layer_norm(own_tokens + sums[0])[0].astype(jnp.bfloat16)
        predicted, factor = layer_norm(own_seeds + sums[1])
        back_grad = gradient(predicted, factor, features, usable)
    back_all = gather_rows(back_grad.astype(jnp.bfloat16), shards)[0]
    head_grad = lax.dot_general(
        student_mixed,
        own_part(back_all),
        (((0,), (0,)), ((), ())),
        preferred_element_type=jnp.float32,
    ).astype(jnp.bfloat16)
    if fused:
        head_grad, target_out, student_out, other_out = lax.optimization_barrier(
            (head_grad, target_out, student_out, other_out)
        )
        relaid = both_of_dp(student_out, 1, other_out)
    if lax.axis_size("dp") == 2:
        half = head_grad.shape[1] // 2
        first = lax.axis_index("dp") == 0
        low, high = head_grad[:, :half], head_grad[:, half:]
        keep, send = jnp.where(first, low, high), jnp.where(first, high, low)
        came = lax.ppermute(send, "dp", [(0, 1), (1, 0)])
        head_grad = (keep.astype(jnp.float32) + came.astype(jnp.float32)).astype(jnp.bfloat16)
    else:
        head_grad = lax.psum_scatter(head_grad, "dp", scatter_dimension=1, tiled=True)
    out_grad = lax.all_gather(head_grad, "seq", axis=0, tiled=True).astype(jnp.float32)
    if rep > 1:
        out_grad = out_grad.reshape(head_count, rep, HEAD_DIM, -1).sum(1)
        out_grad = out_grad.reshape(half_width, -1)
    target_blend = MOMENTUM * target_out.astype(jnp.float32) + (1.0 - MOMENTUM) * relaid.astype(
        jnp.float32
    )
    return (out_grad, target_blend)


def solution(mesh):
    in_specs = (
        P("dp", "seq", None),
        P("dp", "seq"),
        P("dp", "seq"),
        P(None, "dp", "grp"),
        P("grp", None),
        P(None, "dp", "grp"),
        P("grp", "dp"),
        P(),
    )
    out_specs = (P("grp", "dp"), P("grp", None))
    return jax.shard_map(body, mesh=mesh, in_specs=in_specs, out_specs=out_specs, check_vma=False)
```

```python
import functools
import math

import jax
import jax.numpy as jnp
from jax import lax
from jax.experimental import pallas as pl
from jax.experimental.pallas import tpu as pltpu
from jax.sharding import PartitionSpec as P

MESH = pl.DeviceIdType.MESH
CHUNKS = 4

HEAD_DIM = 88
CTX_DEV = 32
EPSILON = 1e-06
MOMENTUM = 0.99
STRIDE = 32


def layer_norm(values):
    center = values - jnp.mean(values, axis=-1, keepdims=True)
    factor = lax.rsqrt(jnp.mean(center * center, axis=-1, keepdims=True) + EPSILON)
    return (center * factor, factor)


def position_tables(length, width):
    half_width = width // 2
    spacing = jnp.exp(jnp.arange(half_width, dtype=jnp.float32) * (-math.log(10000.0) / half_width))
    high = (jnp.arange(length // STRIDE) * STRIDE).astype(jnp.float32)[:, None] * spacing[None, :]
    low = jnp.arange(STRIDE).astype(jnp.float32)[:, None] * spacing[None, :]
    sin_h, cos_h = jnp.sin(high), jnp.cos(high)
    sin_l, cos_l = jnp.sin(low), jnp.cos(low)
    return (
        jnp.concatenate([sin_h, cos_h], axis=1),
        jnp.concatenate([cos_h, -sin_h], axis=1),
        jnp.concatenate([cos_l, cos_l], axis=1),
        jnp.concatenate([sin_l, sin_l], axis=1),
    )


def norm_seed_block(index, tables, mask_ref, seed_out):
    first, second, twice_c, twice_s = tables
    rows = pl.ds(index, 1)
    seeds = mask_ref[...] + (first[rows, :] * twice_c[...] + second[rows, :] * twice_s[...])
    start = pl.multiple_of(index * STRIDE, STRIDE)
    seed_out[pl.ds(start, STRIDE), :] = layer_norm(seeds)[0].astype(jnp.bfloat16)


def gather_kernel(shards, with_seeds, *refs):
    if with_seeds:
        (x_ref, small_ref, *tables, mask_ref, out_ref, small_out, seed_out) = refs[:10]
        sems = refs[10:]
        s_send, s_recv, s_own = sems[7:]
    else:
        x_ref, out_ref = refs[:2]
        sems = refs[2:]
    own_sem, z_send, z_recv, m_send, m_recv, y_send, y_recv = sems[:7]
    me, grp = lax.axis_index("seq"), lax.axis_index("grp")
    z, core = me // 2, me % 2
    depth = shards // 2
    mate, across = z * 2 + (1 - core), 1 - grp
    pieces = range(CHUNKS)

    barrier = pltpu.get_barrier_semaphore()
    if with_seeds:
        for k in range(1, shards):
            peer = {"seq": lax.rem(me + k, shards)}
            pl.semaphore_signal(barrier, inc=1, device_id=peer, device_id_type=MESH)
        greeted = shards - 1
    else:
        for k in range(1, depth):
            peer = {"seq": lax.rem(z + k, depth) * 2 + core}
            pl.semaphore_signal(barrier, inc=1, device_id=peer, device_id_type=MESH)
        pl.semaphore_signal(barrier, inc=1, device_id={"seq": mate}, device_id_type=MESH)
        greeted = depth
    pl.semaphore_signal(barrier, inc=1, device_id={"grp": across}, device_id_type=MESH)
    pl.semaphore_wait(barrier, greeted + 1)

    def remote(src, slot, group, piece, send, recv, to):
        return pltpu.make_async_remote_copy(
            src_ref=src,
            dst_ref=out_ref.at[slot, group, piece],
            send_sem=send,
            recv_sem=recv,
            device_id=to,
            device_id_type=MESH,
        )

    def z_copy(way, dist, piece):
        sign = 1 - 2 * way
        slot = (z - sign * (dist - 1)) * 2 + core
        src = x_ref.at[piece] if dist == 1 else out_ref.at[slot, grp, piece]
        return remote(
            src, slot, grp, piece,
            z_send.at[way, dist - 1, piece], z_recv.at[way, dist - 1, piece],
            {"seq": (z + sign) * 2 + core},
        )

    def comes(way, dist):
        return z >= dist if way == 0 else z + dist < depth

    def leaves(way):
        return z + 1 < depth if way == 0 else z >= 1

    def goes(way, dist):
        return leaves(way) if dist == 1 else leaves(way) & comes(way, dist - 1)

    def mate_copy(src, source, side, piece):
        group = grp if side == 0 else across
        return remote(
            src, source * 2 + core, group, piece,
            m_send.at[side, source, piece], m_recv.at[side, source, piece], {"seq": mate},
        )

    def y_copy(src, source, piece):
        return remote(
            src, source * 2 + core, grp, piece,
            y_send.at[source, piece], y_recv.at[source, piece], {"grp": across},
        )

    def small_copy(k):
        return pltpu.make_async_remote_copy(
            src_ref=small_ref,
            dst_ref=small_out.at[me],
            send_sem=s_send.at[k - 1],
            recv_sem=s_recv.at[k - 1],
            device_id={"seq": lax.rem(me + k, shards)},
            device_id_type=MESH,
        )

    for way in range(2):

        @pl.when(goes(way, 1))
        def _():
            for piece in pieces:
                z_copy(way, 1, piece).start()

    for piece in pieces:
        y_copy(x_ref.at[piece], z, piece).start()
        mate_copy(x_ref.at[piece], z, 0, piece).start()
    own = pltpu.make_async_copy(x_ref, out_ref.at[me, grp], own_sem)
    own.start()
    if with_seeds:
        for k in range(1, shards):
            small_copy(k).start()
        small_own = pltpu.make_async_copy(small_ref, small_out.at[me], s_own)
        small_own.start()
        blocks = seed_out.shape[0] // STRIDE
        stages = depth + 1

    def work(stage):
        if with_seeds:
            lax.fori_loop(
                stage * blocks // stages,
                (stage + 1) * blocks // stages,
                lambda i, _: (norm_seed_block(i, tables, mask_ref, seed_out), 0)[1],
                0,
            )

    def from_z(way, dist):
        source = z - dist if way == 0 else z + dist

        @pl.when(comes(way, dist))
        def _():
            for piece in pieces:
                z_copy(way, dist, piece).wait_recv()
                if dist + 1 < depth:

                    @pl.when(leaves(way))
                    def _():
                        z_copy(way, dist + 1, piece).start()

                held = out_ref.at[source * 2 + core, grp, piece]
                y_copy(held, source, piece).start()
                mate_copy(held, source, 0, piece).start()

    def from_y(source):
        for piece in pieces:
            held = out_ref.at[source * 2 + core, across, piece]
            y_copy(held, source, piece).wait_recv()
            mate_copy(held, source, 1, piece).start()

    work(0)
    from_y(z)
    for dist in range(1, depth):
        work(dist)
        for way in range(2):
            from_z(way, dist)
        if dist > 1:
            for way in range(2):

                @pl.when(comes(way, dist - 1))
                def _():
                    from_y(z - (dist - 1) if way == 0 else z + (dist - 1))

    work(depth)
    for way in range(2):

        @pl.when(comes(way, depth - 1))
        def _():
            from_y(z - (depth - 1) if way == 0 else z + (depth - 1))

    for source in range(depth):
        for piece in pieces:
            for side in range(2):
                mate_copy(out_ref.at[source * 2 + core, grp, piece], source, side, piece).wait()
            y_copy(out_ref.at[source * 2 + core, grp, piece], source, piece).wait_send()
    for dist in range(1, depth):
        for way in range(2):

            @pl.when(goes(way, dist))
            def _():
                for piece in pieces:
                    z_copy(way, dist, piece).wait_send()

    own.wait()
    if with_seeds:
        for k in range(1, shards):
            small_copy(k).wait()
        small_own.wait()


def gather_rows(rows, shards, small=None, tables=None, mask=None):
    count, width = rows.shape
    depth = shards // 2
    dma = pltpu.SemaphoreType.DMA
    shaped = rows.reshape(CHUNKS, count // CHUNKS, width)
    out_shape = [jax.ShapeDtypeStruct((shards, 2) + shaped.shape, rows.dtype)]
    operands = [shaped]
    scratch = [
        dma,
        dma((2, depth - 1, CHUNKS)),
        dma((2, depth - 1, CHUNKS)),
        dma((2, depth, CHUNKS)),
        dma((2, depth, CHUNKS)),
        dma((depth, CHUNKS)),
        dma((depth, CHUNKS)),
    ]
    with_seeds = small is not None
    if with_seeds:
        operands += [small, *tables, mask[None, :]]
        out_shape += [
            jax.ShapeDtypeStruct((shards,) + small.shape, small.dtype),
            jax.ShapeDtypeStruct((tables[0].shape[0] * STRIDE, width), jnp.bfloat16),
        ]
        scratch += [dma((shards - 1,)), dma((shards - 1,)), dma]
    vmem = pl.BlockSpec(memory_space=pltpu.VMEM)
    results = pl.pallas_call(
        functools.partial(gather_kernel, shards, with_seeds),
        out_shape=out_shape,
        in_specs=[vmem] * len(operands),
        out_specs=[vmem] * len(out_shape),
        scratch_shapes=scratch,
        name="gather_seeds" if with_seeds else "gather_rows",
        compiler_params=pltpu.CompilerParams(
            collective_id=1 if with_seeds else 2,
            has_side_effects=True,
            vmem_limit_bytes=48 * 1024 * 1024,
        ),
    )(*operands)
    return (results[0].reshape(shards * 2 * count, width), *results[1:])


def middle_kernel(shards, *refs):
    (
        every, seeded, chosen, weights, out_t, own_s, other_s, tokens_ref, seeds_ref, usable_ref,
        back_ref, mix_s, k_t, v_t, k_s, v_s, mix_t, got_t, got_s, part_t, part_s, came_t, came_s,
        send_t, recv_t, send_s, recv_s, y_send, y_recv,
    ) = refs
    me, grp = lax.axis_index("seq"), lax.axis_index("grp")
    across = 1 - grp

    barrier = pltpu.get_barrier_semaphore()
    for k in range(1, shards):
        peer = {"seq": lax.rem(me + k, shards)}
        pl.semaphore_signal(barrier, inc=1, device_id=peer, device_id_type=MESH)
    pl.semaphore_signal(barrier, inc=1, device_id={"grp": across}, device_id_type=MESH)
    pl.semaphore_wait(barrier, shards)

    def turn(k):
        return lax.rem(me + 1 + k, shards)

    def copy(k, mix, got, send, recv):
        return pltpu.make_async_remote_copy(
            src_ref=mix.at[turn(k)],
            dst_ref=got.at[me],
            send_sem=send.at[k],
            recv_sem=recv.at[k],
            device_id={"seq": turn(k)},
            device_id_type=MESH,
        )

    def narrow(rows, index):
        return dot32(rows, weights[index]).astype(jnp.bfloat16)

    def heads(source, index, keys, values, mix, got, send, recv):
        def step(k, carry):
            dest = turn(k)
            queries = narrow(source[dest], index)
            mix[dest] = attend(queries, keys[...], values[...])

            @pl.when(k > 0)
            def _():
                copy(k - 1, mix, got, send, recv).start()

            return carry

        lax.fori_loop(0, shards, step, 0)
        got[me] = mix[me]

    def y_copy(index, part, came):
        return pltpu.make_async_remote_copy(
            src_ref=part.at[across],
            dst_ref=came,
            send_sem=y_send.at[index],
            recv_sem=y_recv.at[index],
            device_id={"grp": across},
            device_id_type=MESH,
        )

    def joined(got):
        return jnp.concatenate([got[k] for k in range(shards)], axis=1)

    def place(columns, part):
        whole = jnp.concatenate(columns, axis=1).astype(jnp.bfloat16)
        half = whole.shape[0] // 2
        part[0] = whole[:half]
        part[1] = whole[half:]

    def total(part, came):
        return part[grp].astype(jnp.float32) + came[...].astype(jnp.float32)

    def pair(k, carry):
        rows = pl.ds(pl.multiple_of(k * every.shape[1], every.shape[1]), every.shape[1])
        k_t[rows, :] = narrow(every[k], 1)
        v_t[rows, :] = narrow(every[k], 2)
        return carry

    lax.fori_loop(0, shards, pair, 0)
    heads(every, 0, k_t, v_t, mix_t, got_t, send_t, recv_t)
    k_s[...] = narrow(chosen[...], 4)
    v_s[...] = narrow(chosen[...], 5)
    heads(seeded, 3, k_s, v_s, mix_s, got_s, send_s, recv_s)
    for k in range(shards - 1):
        copy(k, mix_t, got_t, send_t, recv_t).wait_recv()
    place([dot32(joined(got_t), out_t[...])], part_t)
    copy(0, mix_s, got_s, send_s, recv_s).wait_recv()
    y_copy(0, part_t, came_t).start()
    for k in range(1, shards - 1):
        copy(k, mix_s, got_s, send_s, recv_s).wait_recv()
    rows = joined(got_s)
    own_columns, other_columns = dot32(rows, own_s[...]), dot32(rows, other_s[...])
    first = lax.axis_index("dp") == 0

    @pl.when(first)
    def _():
        place([own_columns, other_columns], part_s)

    @pl.when(jnp.logical_not(first))
    def _():
        place([other_columns, own_columns], part_s)

    y_copy(0, part_t, came_t).wait_recv()
    y_copy(1, part_s, came_s).start()
    tokens = tokens_ref[...].astype(jnp.float32)
    features = layer_norm(tokens + total(part_t, came_t))[0].astype(jnp.bfloat16)
    y_copy(1, part_s, came_s).wait_recv()
    predicted, factor = layer_norm(seeds_ref[...] + total(part_s, came_s))
    back_ref[...] = gradient(predicted, factor, features, usable_ref[...]).astype(jnp.bfloat16)
    for k in range(shards - 1):
        copy(k, mix_t, got_t, send_t, recv_t).wait_send()
        copy(k, mix_s, got_s, send_s, recv_s).wait_send()
    y_copy(0, part_t, came_t).wait_send()
    y_copy(1, part_s, came_s).wait_send()


def middle(shards, operands):
    blocked = operands[0].shape[:2] + (HEAD_DIM,)
    flat = (blocked[0] * blocked[1], HEAD_DIM)
    some = (operands[2].shape[0], HEAD_DIM)
    rows, width = operands[7].shape
    bf16, dma = jnp.bfloat16, pltpu.SemaphoreType.DMA
    vmem = pl.BlockSpec(memory_space=pltpu.VMEM)
    return pl.pallas_call(
        functools.partial(middle_kernel, shards),
        out_shape=[
            jax.ShapeDtypeStruct((rows, width), bf16),
            jax.ShapeDtypeStruct(blocked, bf16),
        ],
        in_specs=[vmem] * len(operands),
        out_specs=[vmem] * 2,
        scratch_shapes=[pltpu.VMEM(flat, bf16)] * 2
        + [pltpu.VMEM(some, bf16)] * 2
        + [pltpu.VMEM(blocked, bf16)] * 3
        + [pltpu.VMEM((2, rows, width), bf16)] * 2
        + [pltpu.VMEM((rows, width), bf16)] * 2
        + [dma((shards - 1,))] * 4
        + [dma((2,))] * 2,
        name="middle",
        compiler_params=pltpu.CompilerParams(
            collective_id=3, has_side_effects=True, vmem_limit_bytes=48 * 1024 * 1024
        ),
    )(*operands)


def gradient(predicted, factor, features, usable):
    slope = jnp.clip(predicted - features.astype(jnp.float32), -1.0, 1.0) * usable
    return (
        slope
        - jnp.mean(slope, axis=1, keepdims=True)
        - predicted * jnp.mean(slope * predicted, axis=1, keepdims=True)
    ) * factor


def attend(queries, keys, values):
    scores = lax.dot_general(
        queries, keys, (((1,), (1,)), ((), ())), preferred_element_type=jnp.float32
    ) * (HEAD_DIM ** (-0.5))
    shifted = jnp.exp(scores - jnp.max(scores, axis=1, keepdims=True))
    totals = jnp.sum(shifted, axis=1, keepdims=True)
    summed = jnp.dot(shifted.astype(jnp.bfloat16), values, preferred_element_type=jnp.float32)
    return (summed / totals).astype(jnp.bfloat16)


def dot32(left, right):
    return jnp.dot(left, right, preferred_element_type=jnp.float32)


def swap(block):
    return lax.ppermute(block, "dp", [(0, 1), (1, 0)])


def both_of_dp(block, axis, other=None):
    if lax.axis_size("dp") != 2:
        return lax.all_gather(block, "dp", axis=axis, tiled=True)
    if other is None:
        other = swap(block)
    first = lax.axis_index("dp") == 0
    return jnp.concatenate(
        [jnp.where(first, block, other), jnp.where(first, other, block)], axis=axis
    )


def body(
    clips, context, predict_index, target_qkv, target_out, student_qkv, student_out, mask_token
):
    row_count, width = clips.shape[1:]
    half_width = target_qkv.shape[2]
    head_count = half_width // HEAD_DIM
    shards = lax.axis_size("seq")
    rep = shards // head_count
    length = shards * row_count
    me = lax.axis_index("seq")
    head, part = me // rep, me % rep
    part_rows = length // rep

    def columns(weights):
        return lax.dynamic_slice_in_dim(weights, head * HEAD_DIM, HEAD_DIM, axis=2)

    mine = jnp.concatenate([columns(target_qkv), columns(student_qkv)], axis=0)
    weights = both_of_dp(mine, 1)
    fused = rep == 1 and lax.axis_size("dp") == 2
    if fused:
        other_out = swap(student_out)
    else:
        relaid = both_of_dp(student_out, 1)

    grp = lax.axis_index("grp")
    half_rows = row_count // 2
    own_tokens = lax.dynamic_slice_in_dim(clips[0], grp * half_rows, half_rows, axis=0)
    own_tokens = own_tokens.astype(jnp.float32)
    normed = layer_norm(own_tokens)[0].astype(jnp.bfloat16)
    tables = position_tables(length, width)
    small = jnp.concatenate([context[0], predict_index[0]])[None, :]
    small = jnp.pad(small, ((0, 7), (0, -small.shape[1] % 128)))
    every, small, seed_normed = gather_rows(normed, shards, small, tables, mask_token)
    small = small[:, 0]
    flags = small[:, :row_count]
    lists = small[:, row_count : row_count + predict_index.shape[1]].reshape(-1)

    def own_part(rows):
        if rep == 1:
            return rows
        return lax.dynamic_slice_in_dim(rows, part * part_rows, part_rows, axis=0)

    def project(rows, some):
        return jnp.einsum(
            "nr,krc->knc", rows, some, preferred_element_type=jnp.float32
        ).astype(jnp.bfloat16)

    is_context = flags == 1
    order = jnp.cumsum(is_context.astype(jnp.int32), axis=1) - 1
    selector = (
        (order[:, None, :] == jnp.arange(CTX_DEV, dtype=jnp.int32)[None, :, None])
        & is_context[:, None, :]
    ).astype(jnp.bfloat16)
    chosen = jnp.einsum(
        "sck,skw->scw",
        selector,
        every.reshape(shards, row_count, width),
        preferred_element_type=jnp.float32,
    ).astype(jnp.bfloat16)
    chosen = chosen.reshape(shards * CTX_DEV, width)

    base = me * row_count + grp * half_rows
    first, second, twice_c, twice_s = tables
    blocks = half_rows // STRIDE
    first = lax.dynamic_slice_in_dim(first, base // STRIDE, blocks, axis=0)
    second = lax.dynamic_slice_in_dim(second, base // STRIDE, blocks, axis=0)
    own_seeds = first[:, None] * twice_c[None] + second[:, None] * twice_s[None]
    own_seeds = mask_token[None, :] + own_seeds.reshape(half_rows, width)
    places = base + jnp.arange(half_rows, dtype=jnp.int32)
    usable = jnp.sum(
        (lists[None, :] == places[:, None]).astype(jnp.float32), axis=1, keepdims=True
    )
    if fused:
        blocked = (shards, row_count, width)
        back_grad, student_mixed = middle(
            shards,
            [
                every.reshape(blocked), seed_normed.reshape(blocked), chosen, weights,
                target_out, student_out, other_out, own_tokens, own_seeds, usable,
            ],
        )
        student_mixed = student_mixed.reshape(length, HEAD_DIM)
    else:
        query_t = dot32(own_part(every), weights[0]).astype(jnp.bfloat16)
        key_t, value_t = project(every, weights[1:3])
        seed_queries = dot32(own_part(seed_normed), weights[3]).astype(jnp.bfloat16)
        key_s, value_s = project(chosen, weights[4:])
        target_mixed = attend(query_t, key_t, value_t)
        student_mixed = attend(seed_queries, key_s, value_s)
        both = jnp.concatenate([target_mixed, student_mixed], axis=1)
        if rep == 1:
            both = both.reshape(shards, row_count, 2 * HEAD_DIM)
            both = lax.all_to_all(both, "seq", split_axis=0, concat_axis=0, tiled=True)
        else:
            both = lax.all_gather(both, "seq", axis=0, tiled=True)
            both = both.reshape(head_count, length, 2 * HEAD_DIM)
            both = lax.dynamic_slice_in_dim(both, me * row_count, row_count, axis=1)
        own_target = both[:, :, :HEAD_DIM].transpose(1, 0, 2).reshape(row_count, half_width)
        own_student = both[:, :, HEAD_DIM:].transpose(1, 0, 2).reshape(row_count, half_width)
        sums = jnp.stack(
            [
                dot32(own_target, target_out).astype(jnp.bfloat16),
                dot32(own_student, relaid).astype(jnp.bfloat16),
            ]
        )
        low, high = sums[:, :half_rows], sums[:, half_rows:]
        keep, send = jnp.where(grp == 0, low, high), jnp.where(grp == 0, high, low)
        came = lax.ppermute(send, "grp", [(0, 1), (1, 0)])
        sums = keep.astype(jnp.float32) + came.astype(jnp.float32)

        features = layer_norm(own_tokens + sums[0])[0].astype(jnp.bfloat16)
        predicted, factor = layer_norm(own_seeds + sums[1])
        back_grad = gradient(predicted, factor, features, usable)
    back_all = gather_rows(back_grad.astype(jnp.bfloat16), shards)[0]
    head_grad = lax.dot_general(
        student_mixed,
        own_part(back_all),
        (((0,), (0,)), ((), ())),
        preferred_element_type=jnp.float32,
    ).astype(jnp.bfloat16)
    if fused:
        head_grad, target_out, student_out, other_out = lax.optimization_barrier(
            (head_grad, target_out, student_out, other_out)
        )
        relaid = both_of_dp(student_out, 1, other_out)
    if lax.axis_size("dp") == 2:
        half = head_grad.shape[1] // 2
        first = lax.axis_index("dp") == 0
        low, high = head_grad[:, :half], head_grad[:, half:]
        keep, send = jnp.where(first, low, high), jnp.where(first, high, low)
        came = lax.ppermute(send, "dp", [(0, 1), (1, 0)])
        head_grad = (keep.astype(jnp.float32) + came.astype(jnp.float32)).astype(jnp.bfloat16)
    else:
        head_grad = lax.psum_scatter(head_grad, "dp", scatter_dimension=1, tiled=True)
    out_grad = lax.all_gather(head_grad, "seq", axis=0, tiled=True).astype(jnp.float32)
    if rep > 1:
        out_grad = out_grad.reshape(head_count, rep, HEAD_DIM, -1).sum(1)
        out_grad = out_grad.reshape(half_width, -1)
    target_blend = MOMENTUM * target_out.astype(jnp.float32) + (1.0 - MOMENTUM) * relaid.astype(
        jnp.float32
    )
    return (out_grad, target_blend)


def solution(mesh):
    in_specs = (
        P("dp", "seq", None),
        P("dp", "seq"),
        P("dp", "seq"),
        P(None, "dp", "grp"),
        P("grp", None),
        P(None, "dp", "grp"),
        P("grp", "dp"),
        P(),
    )
    out_specs = (P("grp", "dp"), P("grp", None))
    return jax.shard_map(body, mesh=mesh, in_specs=in_specs, out_specs=out_specs, check_vma=False)
```
